512 devices in a mesh: date: 64 (over y, z_lo, x), row: 8 (over z_hi, core).
Axes of the slice: x: 4, y: 8, z: 8 (z_hi: 4, z_lo: 2; z = z_hi * 2 + z_lo), core: 2. Of those that a mesh axis runs over, the one named last changes fastest.
Arguments:
- tokens: bfloat16 [128, 128, 16, 384], P('date', 'row'), may hold values from -6 to 6
- clear_flags: int32 [128, 128, 16], P('date', 'row'), may hold values 0 or 1
- date_numbers: int32 [128], P('date'), may hold values from 0 to 1023, as said below
- decay_slopes: float32 [12], replicated, may hold values from 0.00048828125 to 0.03
- time_project: bfloat16 [384, 1152], replicated, may hold values from -0.35 to 0.35
- time_output: bfloat16 [384, 384], replicated, may hold values from -0.3125 to 0.3125
- column_project: bfloat16 [384, 1152], replicated, may hold values from -0.35 to 0.35
- column_output: bfloat16 [384, 384], replicated, may hold values from -0.3125 to 0.3125
- cotangent: bfloat16 [128, 128, 16, 384], P('date', 'row'), may hold values from -6 to 6
Outputs:
- mixed_tokens: bfloat16 [128, 128, 16, 384], P('date', 'row')
- column_project_grad: float32 [384, 1152], P('row', 'date')
- column_output_grad: float32 [384, 384], P('row', 'date')
The draws below stay inside these ranges and needn't reach their ends.
Inputs may be any that keep to these rules, and one draw needn't show every extreme that they name: `date_numbers`: strictly increasing; consecutive dates lie 1 to 15 days apart.
All inputs are finite; a program needn't handle non-finite values. No bound on the sum of `clear_flags` on one device may be relied on, other than what follows from the above.
Results may differ from the reference program's by a relative error of at most 0.018.
The reference program's roundings to bfloat16 on the way count: a program that leaves them out, or rounds other values in their place, can miss the bound.
Values may be sent and summed in bfloat16 or wider, within the bound.
A program may use at most 64 MiB of HBM per device.

```python
import math
import jax
import jax.numpy as jnp
from jax import lax

D = 384
HEADS = 12
COLS = 16
DATES = 128
ROWS = 128


def draw_date_numbers(key, part):
    jitter = jax.random.randint(jax.random.fold_in(key, 17), (DATES,), 0, 8)
    positions = jnp.arange(DATES, dtype=jnp.int32)
    jitter = jnp.where(positions == 0, 0, jnp.where(positions == DATES - 1, 7, jitter))
    return (positions * 8 + jitter).astype(jnp.int32)


def draw_tokens(key, part):
    noise = jax.random.truncated_normal(jax.random.fold_in(key, 31), -6.0, 6.0, (DATES, ROWS, COLS, D), jnp.float32)
    return noise.astype(jnp.bfloat16)


def projection_draw(key, salt):
    base = jax.random.truncated_normal(jax.random.fold_in(key, salt), -6.0, 6.0, (D, 3 * D), jnp.float32) * D ** (-0.5)
    return jnp.clip(base, -0.35, 0.35)


def draw_time_project(key, part):
    return projection_draw(key, 101).astype(jnp.bfloat16)


def draw_column_project(key, part):
    return projection_draw(key, 202).astype(jnp.bfloat16)


def place_ends(values, stream_key, low, high):
    longest = values.shape.index(max(values.shape))
    spots = []
    for shift in (0, 1):
        where = [jax.random.randint(jax.random.fold_in(stream_key, axis), (), 0, length) for axis, length in enumerate(values.shape)]
        where[longest] = (where[longest] + shift) % values.shape[longest]
        spots.append(tuple(where))
    return values.at[spots[0]].set(low).at[spots[1]].set(high)


def steps_of(own_key, extent, pieces, least, top_value):
    def one(dim, blocks):
        steps = jax.random.uniform(jax.random.fold_in(jax.random.fold_in(own_key, 6), dim), (blocks,), jnp.float32, least / len(pieces), top_value / len(pieces))
        return jnp.repeat(jnp.exp(steps), extent[dim] // blocks).reshape((-1,) + (1,) * (len(extent) - dim - 1))

    loudness = one(*pieces[0])
    for cut in pieces[1:]:
        loudness = loudness * one(*cut)
    return loudness


def bell_draw(key, extent, width, most, split=(), kind=jnp.bfloat16):
    values = width * jax.random.normal(key, extent, jnp.float32)
    if split:
        values = values * steps_of(key, extent, split, -0.22, 0.18)
    return jnp.clip(values, -most, most).astype(kind)


def setup_inputs(seed: int = 0) -> dict:
    arg_keys = jax.random.split(jax.random.key(seed), 10)
    return {
        "tokens": draw_tokens(jax.random.fold_in(arg_keys[9], 71), 0),
        "clear_flags": place_ends((jax.random.randint(arg_keys[1], (DATES, ROWS, COLS), 0, 4) < 3).astype(jnp.int32), jax.random.fold_in(arg_keys[1], 1), 0, 1),
        "date_numbers": draw_date_numbers(jax.random.fold_in(arg_keys[9], 71), 0),
        "decay_slopes": jnp.clip(jnp.exp(jax.random.uniform(arg_keys[3], (HEADS,), jnp.float32, math.log(0.00048828125), math.log(0.03))), 0.00048828125, 0.03),
        "time_project": draw_time_project(jax.random.fold_in(arg_keys[9], 71), 0),
        "time_output": bell_draw(arg_keys[5], (D, D), D ** -0.5, 0.3125),
        "column_project": draw_column_project(jax.random.fold_in(arg_keys[9], 71), 0),
        "column_output": bell_draw(arg_keys[7], (D, D), D ** -0.5, 0.3125),
        "cotangent": bell_draw(arg_keys[8], (DATES, ROWS, COLS, D), 1.0, 6.0, ((0, 64), (1, 8))),
    }


epsilon = 1e-06
masked_score = -1e+30

def rms_norm(values):
    widened = values.astype(jnp.float32)
    factor = lax.rsqrt(lax.optimization_barrier(jnp.mean(widened * widened, axis=-1, keepdims=True)) + epsilon)
    return (widened * factor).astype(jnp.bfloat16)

def softmax_rows(scores):
    top_score = lax.optimization_barrier(jnp.max(scores, axis=-1, keepdims=True))
    raised = jnp.exp(scores - top_score)
    return raised / lax.optimization_barrier(jnp.sum(raised, axis=-1, keepdims=True))

def lowered(values):
    return lax.optimization_barrier(values.astype(jnp.bfloat16)).astype(jnp.float32)

def reference(tokens, clear_flags, date_numbers, decay_slopes, time_project, time_output, column_project, column_output, cotangent):
    head_size = D // HEADS
    inverse_root = 1.0 / math.sqrt(head_size)
    gap_days = jnp.abs(date_numbers[:, None] - date_numbers[None, :]).astype(jnp.float32)
    time_bias = -decay_slopes[:, None, None] * gap_days[None, :, :]
    positions = jnp.arange(DATES)
    same_date = positions[:, None] == positions[None, :]
    patch_tokens = jnp.transpose(tokens.reshape(DATES, ROWS * COLS, D), (1, 0, 2))
    patch_flags = jnp.transpose(clear_flags.reshape(DATES, ROWS * COLS), (1, 0))

    def time_patch(inputs):
        series, flags = inputs
        normed = rms_norm(series)
        projected = lowered(jnp.dot(normed, time_project, preferred_element_type=jnp.float32))
        projected = projected.reshape(DATES, 3, HEADS, head_size)
        scores = jnp.einsum('qhe,khe->hqk', projected[:, 0], projected[:, 1]) * inverse_root + time_bias
        allowed = (flags[None, :] > 0) | same_date
        scores = jnp.where(allowed[None], scores, masked_score)
        weights_low = lowered(softmax_rows(scores))
        time_heads = jnp.einsum('hqk,khe->qhe', weights_low, projected[:, 2]).astype(jnp.bfloat16)
        update = jnp.dot(time_heads.reshape(DATES, D), time_output, preferred_element_type=jnp.float32)
        return (series.astype(jnp.float32) + update).astype(jnp.bfloat16)
    hidden = lax.map(time_patch, (patch_tokens, patch_flags))
    hidden = jnp.transpose(hidden, (1, 0, 2)).reshape(DATES, ROWS, COLS, D)

    def column_date(totals, inputs):
        plane, plane_grad = inputs
        normed = rms_norm(plane).reshape(ROWS * COLS, D)
        projected = lowered(jnp.dot(normed, column_project, preferred_element_type=jnp.float32))
        projected = projected.reshape(ROWS, COLS, 3, HEADS, head_size)
        queries = projected[:, :, 0]
        key_block = projected[:, :, 1]
        value_block = projected[:, :, 2]
        scores = jnp.einsum('ache,bche->chab', queries, key_block) * inverse_root
        weights = softmax_rows(scores)
        weights_low = lowered(weights)
        column_heads = jnp.einsum('chab,bche->ache', weights_low, value_block).astype(jnp.bfloat16)
        heads_flat = column_heads.reshape(ROWS * COLS, D)
        update = jnp.dot(heads_flat, column_output, preferred_element_type=jnp.float32)
        result = (plane.reshape(ROWS * COLS, D).astype(jnp.float32) + update).astype(jnp.bfloat16)
        grad_flat = plane_grad.reshape(ROWS * COLS, D)
        output_term = jnp.dot(heads_flat.T, grad_flat, preferred_element_type=jnp.float32)
        heads_grad = lowered(jnp.dot(grad_flat, column_output.T, preferred_element_type=jnp.float32))
        heads_grad = heads_grad.reshape(ROWS, COLS, HEADS, head_size)
        product_grad = jnp.einsum('ache,bche->chab', heads_grad, value_block)
        score_grad = weights * (product_grad - lax.optimization_barrier(jnp.sum(weights * product_grad, axis=-1, keepdims=True)))
        score_low = lowered(score_grad)
        query_grad = lowered(jnp.einsum('chab,bche->ache', score_low, key_block) * inverse_root)
        key_grad = lowered(jnp.einsum('chab,ache->bche', score_low, queries) * inverse_root)
        value_grad = lowered(jnp.einsum('chab,ache->bche', weights_low, heads_grad))
        qkv_grad = jnp.stack([query_grad, key_grad, value_grad], axis=2).reshape(ROWS * COLS, 3 * D).astype(jnp.bfloat16)
        project_term = jnp.dot(normed.T, qkv_grad, preferred_element_type=jnp.float32)
        return ((totals[0] + project_term, totals[1] + output_term), result.reshape(ROWS, COLS, D))
    start = (jnp.zeros((D, 3 * D), jnp.float32), jnp.zeros((D, D), jnp.float32))
    totals, mixed_tokens = lax.scan(column_date, start, (hidden, cotangent))
    return (mixed_tokens, totals[0], totals[1])
```

```python
import functools
import math

import jax
import jax.numpy as jnp
from jax import lax
from jax.experimental import pallas as pl
from jax.experimental.pallas import tpu as pltpu
from jax.sharding import PartitionSpec as P

MESH = pl.DeviceIdType.MESH
epsilon = 1e-06
masked_score = -1e30
D = 384
HEADS = 12
GROUPS = 3
inverse_root = 1.0 / math.sqrt(D // HEADS)
bf16, f32 = jnp.bfloat16, jnp.float32


def iota(shape, axis):
    return lax.broadcasted_iota(jnp.int32, shape, axis)


def one_hot(source, width):
    lanes = iota((source.shape[0], width), 1)
    return jnp.where(lanes == source, 1.0, 0.0).astype(bf16)


def matmul(left, right):
    return jnp.dot(left, right, preferred_element_type=f32)


def contract_rows(left, right):
    return lax.dot_general(left, right, (((0,), (0,)), ((), ())), preferred_element_type=f32)


def contract_last(left, right):
    return lax.dot_general(left, right, (((1,), (1,)), ((), ())), preferred_element_type=f32)


def rms_norm(values):
    widened = values.astype(f32)
    factor = lax.rsqrt(jnp.mean(widened * widened, axis=-1, keepdims=True) + epsilon)
    return (widened * factor).astype(bf16)


def head_masks():
    lanes = iota((128, 128), 1) >> 5
    return [lanes == head for head in range(4)]


def stacked(block, masks):
    return jnp.concatenate([jnp.where(mask, block, jnp.zeros_like(block)) for mask in masks], axis=0)


def unstacked(blocks, masks):
    total = jnp.where(masks[0], blocks[0:128], 0.0)
    for head in range(1, 4):
        total = jnp.where(masks[head], blocks[128 * head : 128 * head + 128], total)
    return total


def softmax_block(scores):
    raised = jnp.exp(scores - jnp.max(scores, axis=-1, keepdims=True))
    return raised * (1.0 / jnp.sum(raised, axis=-1, keepdims=True))


def signal(device):
    pl.semaphore_signal(
        pltpu.get_barrier_semaphore(), inc=1, device_id=device, device_id_type=MESH
    )


def remote(source, target, send_sem, recv_sem, device):
    return pltpu.make_async_remote_copy(
        src_ref=source,
        dst_ref=target,
        send_sem=send_sem,
        recv_sem=recv_sem,
        device_id=device,
        device_id_type=MESH,
    )


def wait_bytes(ref, sem):
    pltpu.make_async_copy(ref, ref, sem).wait()


def time_kernel(
    tokens_ref, cotangent_ref, flags_ref, project_ref, output_ref, numbers_ref, slopes_ref,
    rb_ref, rc_ref,
    sa, ra, ss, rs, sc, sb, side, gap_ref, info_ref, base, qkv, heads,
    sem,
):
    d, r = lax.axis_index("date"), lax.axis_index("row")
    parity, octet, kk = d % 2, d // 8, (d // 2) % 4

    def greet_same_row(step, carry):
        signal(((d + step) % 64, r))
        return carry

    def greet_targets(step, carry):
        signal((2 * step + parity, octet))
        signal((8 * r + 2 * (step // 8) + parity, step % 8))
        return carry

    def greet_columns(step, carry):
        signal((d - parity + step // 8, step % 8))
        return carry

    lax.fori_loop(1, 64, greet_same_row, 0)
    lax.fori_loop(0, 32, greet_targets, 0)
    lax.fori_loop(0, 16, greet_columns, 0)

    row = iota((512, 1), 0)
    target = row >> 3
    column = (target & 1) * 8 + (target >> 3)
    source = ((row >> 2) & 1) * 256 + (((target >> 1) & 3) * 4 + (row & 3)) * 16 + column
    sa[...] = matmul(one_hot(source, 512), tokens_ref[...]).astype(bf16).reshape(64, 8, D)
    flipped = contract_rows(
        flags_ref[...].astype(f32).astype(bf16), one_hot(iota((32, 1), 0), 128)
    )
    lane = iota((1, 128), 1)
    first, second = numbers_ref[0], numbers_ref[1]
    extra = jnp.where(lane == 32, first // 32, 0) + jnp.where(lane == 33, second // 32, 0)
    extra = extra + jnp.where(lane == 34, first % 32, 0) + jnp.where(lane == 35, second % 32, 0)
    flipped = flipped + extra.astype(f32)
    for index in range(16):
        ss[index] = flipped[index : index + 1]
    source = ((row >> 4) & 1) * 256 + (row & 15) * 16 + (row >> 5)
    sc[...] = matmul(one_hot(source, 512), cotangent_ref[...]).astype(bf16).reshape(32, 16, D)

    pl.semaphore_wait(pltpu.get_barrier_semaphore(), 63 + 64 + 16)

    def send_tokens(step, carry):
        to = (d + step) % 64
        side_of = (to % 2) * 8 + to // 8
        remote(sa.at[to], ra.at[d], sem.at[0], sem.at[1], (to, r)).start()
        remote(ss.at[side_of], rs.at[d], sem.at[2], sem.at[3], (to, r)).start()
        return carry

    lax.fori_loop(1, 64, send_tokens, 0)
    pltpu.make_async_copy(sa.at[d], ra.at[d], sem.at[1]).start()
    pltpu.make_async_copy(ss.at[parity * 8 + octet], rs.at[d], sem.at[3]).start()
    wait_bytes(rs, sem.at[3])
    wait_bytes(ra, sem.at[1])

    own = parity * 8 + r

    def send_cotangent(step, carry):
        to = (own + step) % 16
        for when in range(2):
            remote(
                sc.at[2 * to + when],
                rc_ref.at[2 * parity + when, pl.ds(pl.multiple_of(16 * r, 16), 16)],
                sem.at[4], sem.at[5], (d - parity + to // 8, to % 8),
            ).start()
        return carry

    lax.fori_loop(1, 16, send_cotangent, 0)
    for when in range(2):
        pltpu.make_async_copy(
            sc.at[2 * own + when],
            rc_ref.at[2 * parity + when, pl.ds(pl.multiple_of(16 * r, 16), 16)],
            sem.at[5],
        ).start()

    for index in range(64):
        side[index : index + 1] = rs[index]
    side_low = side[...].astype(bf16)
    info = jnp.zeros((8, 128), f32)
    pick_row, pick_lane = iota((8, 128), 0), iota((8, 128), 1)
    for when in range(2):
        wanted = jnp.where(pick_row < 4, when * 16 + 4 * kk + pick_row, 32 + when + 2 * (pick_row - 4))
        picked = contract_last(jnp.where(pick_lane == wanted, 1.0, 0.0).astype(bf16), side_low)
        spread = jnp.where(iota((64, 128), 1) == 2 * iota((64, 128), 0) + when, 1.0, 0.0).astype(bf16)
        info = info + matmul(picked.astype(bf16), spread)
    info_ref[...] = info
    days = info[4:5] * 32.0 + info[5:6]
    same_date = iota((128, 128), 0) == iota((128, 128), 1)
    days_down = jnp.sum(jnp.where(same_date, days, 0.0), axis=1, keepdims=True)
    gap_ref[...] = jnp.abs(days_down - days)

    source = ((row & 127) >> 1) * 8 + (row & 1) * 4 + (row >> 7)
    ordered = matmul(one_hot(source, 512), ra[...].reshape(512, D)).astype(bf16)
    base[...] = ordered
    qkv[...] = matmul(rms_norm(ordered), project_ref[...]).astype(bf16)

    def time_patch(patch, carry):
        rows = pl.ds(pl.multiple_of(patch * 128, 128), 128)
        masks = head_masks()
        allowed = (info_ref[pl.ds(patch, 1), :] > 0.5) | (iota((128, 128), 0) == iota((128, 128), 1))
        for group in range(GROUPS):
            queries = qkv[rows, 128 * group : 128 * group + 128]
            keys = stacked(qkv[rows, D + 128 * group : D + 128 * group + 128], masks)
            values = stacked(qkv[rows, 2 * D + 128 * group : 2 * D + 128 * group + 128], masks)
            scores = contract_last(queries, keys)
            weights = []
            for head in range(4):
                block = scores[:, 128 * head : 128 * head + 128] * inverse_root
                block = block + (-slopes_ref[4 * group + head]) * gap_ref[...]
                block = jnp.where(allowed, block, masked_score)
                weights.append(softmax_block(block).astype(bf16))
            heads[rows, 128 * group : 128 * group + 128] = matmul(
                jnp.concatenate(weights, axis=1), values
            ).astype(bf16)
        return carry

    lax.fori_loop(0, 4, time_patch, 0)
    hidden = (base[...].astype(f32) + matmul(heads[...], output_ref[...])).astype(bf16)
    source = ((row >> 2) & 3) * 128 + (row >> 4) * 4 + (row & 3)
    sb[...] = matmul(one_hot(source, 512), hidden).astype(bf16).reshape(32, 16, D)

    slot = 4 * r + kk
    home = r == octet

    def send_hidden(step, carry):
        to = (d // 2 + step) % 32
        remote(sb.at[to], rb_ref.at[slot], sem.at[6], sem.at[7], (2 * to + parity, octet)).start()
        return carry

    lax.fori_loop(1, 32, send_hidden, 0)

    @pl.when(home)
    def _():
        pltpu.make_async_copy(sb.at[d // 2], rb_ref.at[slot], sem.at[7]).start()

    @pl.when(jnp.logical_not(home))
    def _():
        remote(sb.at[d // 2], rb_ref.at[slot], sem.at[6], sem.at[7], (d, octet)).start()

    wait_bytes(rb_ref, sem.at[7])
    wait_bytes(rc_ref, sem.at[5])
    wait_bytes(sa.at[pl.ds(0, 63)], sem.at[0])
    wait_bytes(rs.at[pl.ds(0, 63)], sem.at[2])
    wait_bytes(sc.at[pl.ds(0, 30)], sem.at[4])
    wait_bytes(sb.at[pl.ds(0, 31)], sem.at[6])

    @pl.when(jnp.logical_not(home))
    def _():
        wait_bytes(sb.at[0], sem.at[6])


def column_kernel(
    rb_ref, rc_ref, project_ref, output_ref,
    mixed_ref, project_grad_ref, output_grad_ref,
    plane, normed, qkv, heads_grad, heads, qkv_grad, send_c, recv_c, natural, partial,
    s1, r1, s2, r2, s3, r3, s4, r4,
    sem,
):
    d, r = lax.axis_index("date"), lax.axis_index("row")
    parity, octet = d % 2, d // 8
    x, z_lo, core = d % 4, (d // 4) % 2, r % 2
    own = parity * 8 + r
    partner = (d, r + 1 - 2 * core)

    def greet_rows(step, carry):
        to = (own + step) % 16
        signal((d - parity + to // 8, to % 8))
        return carry

    lax.fori_loop(1, 16, greet_rows, 0)
    signal(partner)
    for step in range(1, 4):
        signal((d - x + (x + step) % 4, r))
    for step in range(1, 8):
        signal(((d + 8 * step) % 64, r))
    for index in range(8):
        signal((d - 4 * z_lo + 4 * core, index))
        signal((d - 4 * z_lo + 4 * (index % 2), index - index % 2 + z_lo))

    row = iota((512, 1), 0)
    source = ((row & 127) >> 2) * 16 + (row & 3) * 4 + (row >> 7)
    hidden = matmul(one_hot(source, 512), rb_ref[...].reshape(512, D)).astype(bf16)
    plane[...] = hidden
    column_normed = rms_norm(hidden)
    normed[...] = column_normed
    qkv[...] = matmul(column_normed, project_ref[...]).astype(bf16)
    heads_grad[...] = contract_last(rc_ref[...].reshape(512, D), output_ref[...]).astype(bf16)

    pl.semaphore_wait(pltpu.get_barrier_semaphore(), 15 + 1 + 3 + 7 + 16)

    def column_date(date, carry):
        rows = pl.ds(pl.multiple_of(date * 128, 128), 128)
        masks = head_masks()
        for group in range(GROUPS):
            lanes = slice(128 * group, 128 * group + 128)
            queries = qkv[rows, 128 * group : 128 * group + 128]
            keys = stacked(qkv[rows, D + 128 * group : D + 128 * group + 128], masks)
            values = stacked(qkv[rows, 2 * D + 128 * group : 2 * D + 128 * group + 128], masks)
            outer = heads_grad[rows, lanes]
            scores = contract_last(queries, keys)
            products = contract_last(outer, values)
            weights_low, scores_low = [], []
            for head in range(4):
                weights = softmax_block(scores[:, 128 * head : 128 * head + 128] * inverse_root)
                product = products[:, 128 * head : 128 * head + 128]
                centre = jnp.sum(weights * product, axis=-1, keepdims=True)
                weights_low.append(weights.astype(bf16))
                scores_low.append((weights * (product - centre)).astype(bf16))
            low = jnp.concatenate(weights_low, axis=1)
            score_low = jnp.concatenate(scores_low, axis=1)
            heads[rows, lanes] = matmul(low, values).astype(bf16)
            qkv_grad[rows, 128 * group : 128 * group + 128] = (
                matmul(score_low, keys) * inverse_root
            ).astype(bf16)
            qkv_grad[rows, D + 128 * group : D + 128 * group + 128] = (
                unstacked(contract_rows(score_low, queries), masks) * inverse_root
            ).astype(bf16)
            qkv_grad[rows, 2 * D + 128 * group : 2 * D + 128 * group + 128] = unstacked(
                contract_rows(low, outer), masks
            ).astype(bf16)
        mixed = plane[rows, :].astype(f32) + matmul(heads[rows, :], output_ref[...])
        send_c[date] = mixed.astype(bf16).reshape(8, 16, D)
        to_date = d - parity + date // 2

        def send_rows(step, inner):
            to = (r + step) % 8
            remote(
                send_c.at[date, to], recv_c.at[date % 2, own], sem.at[0], sem.at[1], (to_date, to)
            ).start()
            return inner

        lax.fori_loop(1, 8, send_rows, 0)

        @pl.when(to_date == d)
        def _():
            pltpu.make_async_copy(send_c.at[date, r], recv_c.at[date % 2, own], sem.at[1]).start()

        @pl.when(to_date != d)
        def _():
            remote(
                send_c.at[date, r], recv_c.at[date % 2, own], sem.at[0], sem.at[1], (to_date, r)
            ).start()

        return carry

    lax.fori_loop(0, 4, column_date, 0)

    natural[0:1152] = contract_rows(qkv_grad[...], normed[...])
    natural[1152:1536] = contract_rows(rc_ref[...].reshape(512, D), heads[...])
    for block in range(64):
        bits = (block % 8) * 8 + (block // 32) * 4 + (block // 8) % 4
        partial[block, 0:18] = natural[18 * bits : 18 * bits + 18]
        partial[block, 18:24] = natural[1152 + 6 * bits : 1152 + 6 * bits + 6]

    for chunk in range(3):
        lanes = slice(128 * chunk, 128 * chunk + 128)
        other = partial[pl.ds(pl.multiple_of(32 - 32 * core, 32), 32), :, lanes]
        s1[chunk] = other.reshape(768, 128).astype(bf16)
        remote(s1.at[chunk], r1.at[chunk], sem.at[2 + chunk], sem.at[5 + chunk], partner).start()
    for chunk in range(3):
        lanes = slice(128 * chunk, 128 * chunk + 128)
        mine = partial[pl.ds(pl.multiple_of(32 * core, 32), 32), :, lanes].reshape(768, 128)
        wait_bytes(r1.at[chunk], sem.at[5 + chunk])
        s2[chunk] = (mine + r1[chunk].astype(f32)).astype(bf16).reshape(4, 192, 128)
        for step in range(1, 4):
            to = (x + step) % 4
            remote(
                s2.at[chunk, to], r2.at[chunk, step - 1], sem.at[8 + chunk], sem.at[11 + chunk],
                (d - x + to, r),
            ).start()
    for chunk in range(3):
        wait_bytes(r2.at[chunk], sem.at[11 + chunk])
        total = s2[chunk, x].astype(f32)
        for step in range(3):
            total = total + r2[chunk, step].astype(f32)
        s3[chunk] = total.reshape(8, 24, 128).astype(bf16)
        for step in range(1, 8):
            to = (octet + step) % 8
            remote(
                s3.at[chunk, to], r3.at[chunk, step - 1], sem.at[14 + chunk], sem.at[17 + chunk],
                ((d + 8 * step) % 64, r),
            ).start()
    for chunk in range(3):
        wait_bytes(r3.at[chunk], sem.at[17 + chunk])
        total = s3[chunk, octet].astype(f32)
        for step in range(7):
            total = total + r3[chunk, step].astype(f32)
        square = jnp.concatenate([total, jnp.zeros((104, 128), f32)], axis=0)
        s4[128 * chunk : 128 * chunk + 128] = jnp.transpose(square).astype(bf16)
    z_slot = (r // 2) * 2 + z_lo
    final_date = d - 4 * z_lo + 4 * core

    def send_final(index, carry):
        to = (r + index) % 8
        remote(
            s4.at[pl.ds(pl.multiple_of(48 * to, 16), 48)], r4.at[z_slot], sem.at[20], sem.at[21],
            (final_date, to),
        ).start()
        return carry

    lax.fori_loop(1, 8, send_final, 0)
    mine_last = s4.at[pl.ds(pl.multiple_of(48 * r, 16), 48)]

    @pl.when(final_date == d)
    def _():
        pltpu.make_async_copy(mine_last, r4.at[z_slot], sem.at[21]).start()

    @pl.when(final_date != d)
    def _():
        remote(mine_last, r4.at[z_slot], sem.at[20], sem.at[21], (final_date, r)).start()

    wait_bytes(recv_c, sem.at[1])
    source = ((row >> 8) * 256) + (row & 15) * 16 + ((row >> 4) & 15)
    mixed_ref[...] = matmul(one_hot(source, 512), recv_c[...].reshape(512, D)).astype(bf16)

    wait_bytes(r4, sem.at[21])
    total = r4[0].astype(f32)
    for index in range(1, 8):
        total = total + r4[index].astype(f32)
    project_grad_ref[...] = total[:, 0:18]
    output_grad_ref[...] = total[:, 18:24]

    wait_bytes(send_c.at[pl.ds(0, 3)], sem.at[0])
    wait_bytes(send_c.at[3, pl.ds(0, 6)], sem.at[0])
    for chunk in range(3):
        wait_bytes(s1.at[chunk], sem.at[2 + chunk])
        wait_bytes(s2.at[chunk, pl.ds(0, 3)], sem.at[8 + chunk])
        wait_bytes(s3.at[chunk, pl.ds(0, 7)], sem.at[14 + chunk])
    wait_bytes(r4.at[pl.ds(0, 7)], sem.at[20])

    @pl.when(final_date != d)
    def _():
        wait_bytes(r4.at[0], sem.at[20])


VM = pl.BlockSpec(memory_space=pltpu.VMEM)
SM = pl.BlockSpec(memory_space=pltpu.SMEM)


def body(
    tokens, clear_flags, date_numbers, decay_slopes, time_project, time_output,
    column_project, column_output, cotangent,
):
    rb, rc = pl.pallas_call(
        time_kernel,
        out_shape=(
            jax.ShapeDtypeStruct((32, 16, D), bf16),
            jax.ShapeDtypeStruct((4, 128, D), bf16),
        ),
        in_specs=[VM] * 5 + [SM] * 2,
        out_specs=(VM, VM),
        scratch_shapes=[
            pltpu.VMEM((64, 8, D), bf16),
            pltpu.VMEM((64, 8, D), bf16),
            pltpu.VMEM((16, 1, 128), f32),
            pltpu.VMEM((64, 1, 128), f32),
            pltpu.VMEM((32, 16, D), bf16),
            pltpu.VMEM((32, 16, D), bf16),
            pltpu.VMEM((64, 128), f32),
            pltpu.VMEM((128, 128), f32),
            pltpu.VMEM((8, 128), f32),
            pltpu.VMEM((512, D), bf16),
            pltpu.VMEM((512, 3 * D), bf16),
            pltpu.VMEM((512, D), bf16),
            pltpu.SemaphoreType.DMA((8,)),
        ],
        compiler_params=pltpu.CompilerParams(
            collective_id=0, has_side_effects=True, vmem_limit_bytes=48 * 1024 * 1024
        ),
        name="time_phase",
    )(
        tokens.reshape(512, D), cotangent.reshape(512, D), clear_flags.reshape(32, 16),
        time_project, time_output, date_numbers, decay_slopes,
    )
    mixed, project_grad, output_grad = pl.pallas_call(
        column_kernel,
        out_shape=(
            jax.ShapeDtypeStruct((512, D), bf16),
            jax.ShapeDtypeStruct((48, 18), f32),
            jax.ShapeDtypeStruct((48, 6), f32),
        ),
        in_specs=[VM] * 4,
        out_specs=(VM, VM, VM),
        scratch_shapes=[
            pltpu.VMEM((512, D), bf16),
            pltpu.VMEM((512, D), bf16),
            pltpu.VMEM((512, 3 * D), bf16),
            pltpu.VMEM((512, D), bf16),
            pltpu.VMEM((512, D), bf16),
            pltpu.VMEM((512, 3 * D), bf16),
            pltpu.VMEM((4, 8, 16, D), bf16),
            pltpu.VMEM((2, 16, 16, D), bf16),
            pltpu.VMEM((1536, D), f32),
            pltpu.VMEM((64, 24, D), f32),
            pltpu.VMEM((3, 768, 128), bf16),
            pltpu.VMEM((3, 768, 128), bf16),
            pltpu.VMEM((3, 4, 192, 128), bf16),
            pltpu.VMEM((3, 3, 192, 128), bf16),
            pltpu.VMEM((3, 8, 24, 128), bf16),
            pltpu.VMEM((3, 7, 24, 128), bf16),
            pltpu.VMEM((D, 128), bf16),
            pltpu.VMEM((8, 48, 128), bf16),
            pltpu.SemaphoreType.DMA((22,)),
        ],
        compiler_params=pltpu.CompilerParams(
            collective_id=1, has_side_effects=True, vmem_limit_bytes=48 * 1024 * 1024
        ),
        name="column_phase",
    )(rb, rc, column_project, column_output)
    return mixed.reshape(tokens.shape), project_grad, output_grad


def solution(mesh):
    return jax.shard_map(
        body,
        mesh=mesh,
        in_specs=(
            P("date", "row", None, None), P("date", "row", None), P("date"),
            P(), P(), P(), P(), P(), P("date", "row", None, None),
        ),
        out_specs=(P("date", "row", None, None), P("row", "date"), P("row", "date")),
        check_vma=False,
    )
```

```python
import functools
import math

import jax
import jax.numpy as jnp
from jax import lax
from jax.experimental import pallas as pl
from jax.experimental.pallas import tpu as pltpu
from jax.sharding import PartitionSpec as P

MESH = pl.DeviceIdType.MESH
epsilon = 1e-06
masked_score = -1e30
D = 384
HEADS = 12
GROUPS = 3
inverse_root = 1.0 / math.sqrt(D // HEADS)
bf16, f32 = jnp.bfloat16, jnp.float32


def iota(shape, axis):
    return lax.broadcasted_iota(jnp.int32, shape, axis)


def one_hot(source, width):
    lanes = iota((source.shape[0], width), 1)
    return jnp.where(lanes == source, 1.0, 0.0).astype(bf16)


def matmul(left, right):
    return jnp.dot(left, right, preferred_element_type=f32)


def contract_rows(left, right):
    return lax.dot_general(left, right, (((0,), (0,)), ((), ())), preferred_element_type=f32)


def contract_last(left, right):
    return lax.dot_general(left, right, (((1,), (1,)), ((), ())), preferred_element_type=f32)


def rms_norm(values):
    widened = values.astype(f32)
    factor = lax.rsqrt(jnp.mean(widened * widened, axis=-1, keepdims=True) + epsilon)
    return (widened * factor).astype(bf16)


def head_masks():
    lanes = iota((128, 128), 1) >> 5
    return [lanes == head for head in range(4)]


def stacked(block, masks):
    return jnp.concatenate([jnp.where(mask, block, jnp.zeros_like(block)) for mask in masks], axis=0)


def unstacked(blocks, masks):
    total = jnp.where(masks[0], blocks[0:128], 0.0)
    for head in range(1, 4):
        total = jnp.where(masks[head], blocks[128 * head : 128 * head + 128], total)
    return total


def softmax_block(scores):
    raised = jnp.exp(scores - jnp.max(scores, axis=-1, keepdims=True))
    return raised * (1.0 / jnp.sum(raised, axis=-1, keepdims=True))


def signal(device):
    pl.semaphore_signal(
        pltpu.get_barrier_semaphore(), inc=1, device_id=device, device_id_type=MESH
    )


def remote(source, target, send_sem, recv_sem, device):
    return pltpu.make_async_remote_copy(
        src_ref=source,
        dst_ref=target,
        send_sem=send_sem,
        recv_sem=recv_sem,
        device_id=device,
        device_id_type=MESH,
    )


def wait_bytes(ref, sem):
    pltpu.make_async_copy(ref, ref, sem).wait()


def swing(step, count):
    half = (step + 1) // 2
    return jnp.where(step % 2 == 1, half, count - half)


def layer_kernel(
    tokens_hbm, cotangent_hbm, flags_hbm, time_project_hbm, time_output_hbm,
    column_project_hbm, column_output_hbm, numbers_hbm, slopes_hbm,
    recv_c, r4,
    tokens_ref, rc_in, flags_ref, project_ref, output_ref, column_project_ref, column_output_ref,
    numbers_ref, slopes_ref,
    sa, ra, ss, rs, sc, sb, rb_ref, rc_ref, side, gap_ref, info_ref, base, qkv, heads,
    plane, normed, heads_grad, qkv_grad, send_c, natural, partial_x, partial_y,
    s1, r1, s2x, r2x, s3x, r3x, s2y, r2y, s3y, r3y, s4,
    sem, grad_sem, load_sem,
):
    d, r = lax.axis_index("date"), lax.axis_index("row")
    parity, octet, kk = d % 2, d // 8, (d // 2) % 4
    x, z_lo, core = d % 4, (d // 4) % 2, r % 2
    own = parity * 8 + r
    partner = (d, r + 1 - 2 * core)

    loads = [
        pltpu.make_async_copy(source, target, load_sem.at[index])
        for index, (source, target) in enumerate((
            (tokens_hbm, tokens_ref), (flags_hbm, flags_ref), (numbers_hbm, numbers_ref),
            (cotangent_hbm, rc_in), (time_project_hbm, project_ref), (slopes_hbm, slopes_ref),
            (time_output_hbm, output_ref), (column_output_hbm, column_output_ref),
            (column_project_hbm, column_project_ref),
        ))
    ]
    for load in loads:
        load.start()

    def greet_same_row(step, carry):
        signal(((d + step) % 64, r))
        return carry

    def greet_targets(step, carry):
        signal((2 * step + parity, octet))
        signal((8 * r + 2 * (step // 8) + parity, step % 8))
        return carry

    def greet_columns(step, carry):
        to = (own + step) % 16
        signal((d - parity + to // 8, to % 8))
        return carry

    lax.fori_loop(1, 64, greet_same_row, 0)
    lax.fori_loop(0, 32, greet_targets, 0)
    lax.fori_loop(1, 16, greet_columns, 0)
    signal(partner)
    for index in range(8):
        signal((d - 4 * z_lo + 4 * core, index))
        signal((d - 4 * z_lo + 4 * (index % 2), index - index % 2 + z_lo))

    row = iota((512, 1), 0)
    loads[0].wait()
    target = row >> 3
    column = (target & 1) * 8 + (target >> 3)
    source = ((row >> 2) & 1) * 256 + (((target >> 1) & 3) * 4 + (row & 3)) * 16 + column
    sa[...] = matmul(one_hot(source, 512), tokens_ref[...]).astype(bf16).reshape(64, 8, D)
    loads[1].wait()
    flipped = contract_rows(
        flags_ref[...].astype(f32).astype(bf16), one_hot(iota((32, 1), 0), 128)
    )
    loads[2].wait()
    lane = iota((1, 128), 1)
    first, second = numbers_ref[0], numbers_ref[1]
    extra = jnp.where(lane == 32, first // 32, 0) + jnp.where(lane == 33, second // 32, 0)
    extra = extra + jnp.where(lane == 34, first % 32, 0) + jnp.where(lane == 35, second % 32, 0)
    flipped = flipped + extra.astype(f32)
    for index in range(16):
        ss[index] = flipped[index : index + 1]

    pl.semaphore_wait(pltpu.get_barrier_semaphore(), 63 + 64 + 15 + 1 + 16)

    def send_tokens(step, carry):
        to = (d + swing(step, 64)) % 64
        remote(sa.at[to], ra.at[d], sem.at[0], sem.at[1], (to, r)).start()
        return carry

    def send_side(step, carry):
        to = (d + swing(step, 64)) % 64
        side_of = (to % 2) * 8 + to // 8
        remote(ss.at[side_of], rs.at[d], sem.at[2], sem.at[3], (to, r)).start()
        return carry

    def send_cotangent(step, carry):
        to = (own + step) % 16
        for when in range(2):
            remote(
                sc.at[2 * to + when],
                rc_ref.at[2 * parity + when, pl.ds(pl.multiple_of(16 * r, 16), 16)],
                sem.at[4], sem.at[5], (d - parity + to // 8, to % 8),
            ).start()
        return carry

    lax.fori_loop(1, 64, send_tokens, 0)
    pltpu.make_async_copy(sa.at[d], ra.at[d], sem.at[1]).start()
    lax.fori_loop(1, 64, send_side, 0)
    pltpu.make_async_copy(ss.at[parity * 8 + octet], rs.at[d], sem.at[3]).start()
    loads[3].wait()
    source = ((row >> 4) & 1) * 256 + (row & 15) * 16 + (row >> 5)
    sc[...] = matmul(one_hot(source, 512), rc_in[...]).astype(bf16).reshape(32, 16, D)
    lax.fori_loop(1, 16, send_cotangent, 0)
    for when in range(2):
        pltpu.make_async_copy(
            sc.at[2 * own + when],
            rc_ref.at[2 * parity + when, pl.ds(pl.multiple_of(16 * r, 16), 16)],
            sem.at[5],
        ).start()
    for load in loads[4:]:
        load.wait()

    wait_bytes(ra, sem.at[1])
    source = ((row & 127) >> 1) * 8 + (row & 1) * 4 + (row >> 7)
    ordered = matmul(one_hot(source, 512), ra[...].reshape(512, D)).astype(bf16)
    base[...] = ordered
    qkv[...] = matmul(rms_norm(ordered), project_ref[...]).astype(bf16)

    wait_bytes(rs, sem.at[3])
    for index in range(64):
        side[index : index + 1] = rs[index]
    side_low = side[...].astype(bf16)
    info = jnp.zeros((8, 128), f32)
    pick_row, pick_lane = iota((8, 128), 0), iota((8, 128), 1)
    for when in range(2):
        wanted = jnp.where(pick_row < 4, when * 16 + 4 * kk + pick_row, 32 + when + 2 * (pick_row - 4))
        picked = contract_last(jnp.where(pick_lane == wanted, 1.0, 0.0).astype(bf16), side_low)
        spread = jnp.where(iota((64, 128), 1) == 2 * iota((64, 128), 0) + when, 1.0, 0.0).astype(bf16)
        info = info + matmul(picked.astype(bf16), spread)
    info_ref[...] = info
    days = info[4:5] * 32.0 + info[5:6]
    same_date = iota((128, 128), 0) == iota((128, 128), 1)
    days_down = jnp.sum(jnp.where(same_date, days, 0.0), axis=1, keepdims=True)
    gap_ref[...] = jnp.abs(days_down - days)

    def time_patch(patch, carry):
        rows = pl.ds(pl.multiple_of(patch * 128, 128), 128)
        masks = head_masks()
        allowed = (info_ref[pl.ds(patch, 1), :] > 0.5) | (iota((128, 128), 0) == iota((128, 128), 1))
        for group in range(GROUPS):
            queries = qkv[rows, 128 * group : 128 * group + 128]
            keys = stacked(qkv[rows, D + 128 * group : D + 128 * group + 128], masks)
            values = stacked(qkv[rows, 2 * D + 128 * group : 2 * D + 128 * group + 128], masks)
            scores = contract_last(queries, keys)
            weights = []
            for head in range(4):
                block = scores[:, 128 * head : 128 * head + 128] * inverse_root
                block = block + (-slopes_ref[4 * group + head]) * gap_ref[...]
                block = jnp.where(allowed, block, masked_score)
                weights.append(softmax_block(block).astype(bf16))
            heads[rows, 128 * group : 128 * group + 128] = matmul(
                jnp.concatenate(weights, axis=1), values
            ).astype(bf16)
        return carry

    slot = 2 * (4 * r + kk)
    home = r == octet

    def time_half(half, carry):
        lax.fori_loop(2 * half, 2 * half + 2, time_patch, 0)
        rows = pl.ds(pl.multiple_of(half * 256, 256), 256)
        hidden = (base[rows, :].astype(f32) + matmul(heads[rows, :], output_ref[...])).astype(bf16)
        small = iota((256, 1), 0)
        source = ((small >> 2) & 1) * 128 + (small >> 3) * 4 + (small & 3)
        sb[half] = matmul(one_hot(source, 256), hidden).astype(bf16).reshape(32, 8, D)

        def send_hidden(step, inner):
            to = (d // 2 + swing(step, 32)) % 32
            remote(
                sb.at[half, to], rb_ref.at[slot + half], sem.at[6], sem.at[7],
                (2 * to + parity, octet),
            ).start()
            return inner

        lax.fori_loop(1, 32, send_hidden, 0)

        @pl.when(home)
        def _():
            pltpu.make_async_copy(sb.at[half, d // 2], rb_ref.at[slot + half], sem.at[7]).start()

        @pl.when(jnp.logical_not(home))
        def _():
            remote(
                sb.at[half, d // 2], rb_ref.at[slot + half], sem.at[6], sem.at[7], (d, octet)
            ).start()

        return carry

    lax.fori_loop(0, 2, time_half, 0)

    wait_bytes(rc_ref, sem.at[5])
    heads_grad[...] = contract_last(rc_ref[...].reshape(512, D), column_output_ref[...]).astype(bf16)
    wait_bytes(rb_ref, sem.at[7])

    source = ((row & 127) >> 2) * 16 + (row & 3) * 4 + (row >> 7)
    hidden = matmul(one_hot(source, 512), rb_ref[...].reshape(512, D)).astype(bf16)
    plane[...] = hidden
    column_normed = rms_norm(hidden)
    normed[...] = column_normed
    qkv[...] = matmul(column_normed, column_project_ref[...]).astype(bf16)

    def column_date(date, carry):
        rows = pl.ds(pl.multiple_of(date * 128, 128), 128)
        masks = head_masks()
        for group in range(GROUPS):
            lanes = slice(128 * group, 128 * group + 128)
            queries = qkv[rows, 128 * group : 128 * group + 128]
            keys = stacked(qkv[rows, D + 128 * group : D + 128 * group + 128], masks)
            values = stacked(qkv[rows, 2 * D + 128 * group : 2 * D + 128 * group + 128], masks)
            outer = heads_grad[rows, lanes]
            scores = contract_last(queries, keys)
            products = contract_last(outer, values)
            weights_low, scores_low = [], []
            for head in range(4):
                weights = softmax_block(scores[:, 128 * head : 128 * head + 128] * inverse_root)
                product = products[:, 128 * head : 128 * head + 128]
                centre = jnp.sum(weights * product, axis=-1, keepdims=True)
                weights_low.append(weights.astype(bf16))
                scores_low.append((weights * (product - centre)).astype(bf16))
            low = jnp.concatenate(weights_low, axis=1)
            score_low = jnp.concatenate(scores_low, axis=1)
            heads[rows, lanes] = matmul(low, values).astype(bf16)
            qkv_grad[rows, 128 * group : 128 * group + 128] = (
                matmul(score_low, keys) * inverse_root
            ).astype(bf16)
            qkv_grad[rows, D + 128 * group : D + 128 * group + 128] = (
                unstacked(contract_rows(score_low, queries), masks) * inverse_root
            ).astype(bf16)
            qkv_grad[rows, 2 * D + 128 * group : 2 * D + 128 * group + 128] = unstacked(
                contract_rows(low, outer), masks
            ).astype(bf16)
        mixed = plane[rows, :].astype(f32) + matmul(heads[rows, :], column_output_ref[...])
        send_c[date] = mixed.astype(bf16).reshape(8, 16, D)
        to_date = d - parity + date // 2

        def send_rows(step, inner):
            to = (r + swing(step, 8)) % 8
            remote(
                send_c.at[date, to], recv_c.at[date % 2, own], sem.at[8], sem.at[9], (to_date, to)
            ).start()
            return inner

        lax.fori_loop(1, 8, send_rows, 0)

        @pl.when(to_date == d)
        def _():
            pltpu.make_async_copy(send_c.at[date, r], recv_c.at[date % 2, own], sem.at[9]).start()

        @pl.when(to_date != d)
        def _():
            remote(
                send_c.at[date, r], recv_c.at[date % 2, own], sem.at[8], sem.at[9], (to_date, r)
            ).start()

        return carry

    lax.fori_loop(0, 4, column_date, 0)

    natural[0:1152] = contract_rows(qkv_grad[...], normed[...])
    natural[1152:1536] = contract_rows(rc_ref[...].reshape(512, D), heads[...])
    for block in range(64):
        bits = (block % 8) * 8 + (block // 32) * 4 + (block // 8) % 4
        flipped_block = (block // 32) * 32 + (block % 8) * 4 + (block // 8) % 4
        partial_y[flipped_block, 0:18] = natural[18 * bits : 18 * bits + 18, 256:384]
        partial_y[flipped_block, 18:24] = natural[1152 + 6 * bits : 1152 + 6 * bits + 6, 256:384]
        partial_x[block, 0:18] = natural[18 * bits : 18 * bits + 18, 0:256]
        partial_x[block, 18:24] = natural[1152 + 6 * bits : 1152 + 6 * bits + 6, 0:256]

    along_x = (x, 4, 1, (1, 3, 2), lambda step: (d - x + (x + step) % 4, r))
    along_y = (octet, 8, 8, (1, 7, 2, 6, 3, 5, 4), lambda step: ((d + 8 * step) % 64, r))
    plans = (
        (2, partial_y, 0, along_y, s2y, r2y, along_x, s3y, r3y),
        (0, partial_x, 0, along_x, s2x.at[0], r2x.at[0], along_y, s3x.at[0], r3x.at[0]),
        (1, partial_x, 128, along_x, s2x.at[1], r2x.at[1], along_y, s3x.at[1], r3x.at[1]),
    )

    def exchange(axis, sent, received, send_sem, recv_sem):
        me, size, _, steps, device = axis
        for step in steps:
            remote(
                sent.at[(me + step) % size], received.at[step - 1], send_sem, recv_sem, device(step)
            ).start()

    def gathered(axis, sent, received, recv_sem):
        me, size = axis[:2]
        wait_bytes(received, recv_sem)
        total = sent[me].astype(f32)
        for index in range(size - 1):
            total = total + received[index].astype(f32)
        return total

    for chunk, partial, low, *_ in plans:
        other = partial[pl.ds(pl.multiple_of(32 - 32 * core, 32), 32), :, low : low + 128]
        s1[chunk] = other.reshape(768, 128).astype(bf16)
        remote(
            s1.at[chunk], r1.at[chunk], grad_sem.at[chunk], grad_sem.at[3 + chunk], partner
        ).start()
    for chunk, partial, low, first_axis, sent, received, *_ in plans:
        mine = partial[pl.ds(pl.multiple_of(32 * core, 32), 32), :, low : low + 128].reshape(768, 128)
        wait_bytes(r1.at[chunk], grad_sem.at[3 + chunk])
        size = first_axis[1]
        sent[...] = (mine + r1[chunk].astype(f32)).astype(bf16).reshape(size, 768 // size, 128)
        exchange(first_axis, sent, received, grad_sem.at[6 + chunk], grad_sem.at[9 + chunk])
    for chunk, _, _, first_axis, sent, received, second_axis, sent_next, received_next in plans:
        total = gathered(first_axis, sent, received, grad_sem.at[9 + chunk])
        sent_next[...] = total.reshape(second_axis[1], 24, 128).astype(bf16)
        exchange(
            second_axis, sent_next, received_next, grad_sem.at[12 + chunk], grad_sem.at[15 + chunk]
        )
    for chunk, _, _, _, _, _, second_axis, sent_next, received_next in plans:
        total = gathered(second_axis, sent_next, received_next, grad_sem.at[15 + chunk])
        square = jnp.concatenate([total, jnp.zeros((104, 128), f32)], axis=0)
        s4[128 * chunk : 128 * chunk + 128] = jnp.transpose(square).astype(bf16)
    z_slot = (r // 2) * 2 + z_lo
    final_date = d - 4 * z_lo + 4 * core

    def send_final(step, carry):
        to = (r + swing(step, 8)) % 8
        remote(
            s4.at[pl.ds(pl.multiple_of(48 * to, 16), 48)], r4.at[z_slot],
            grad_sem.at[18], grad_sem.at[19], (final_date, to),
        ).start()
        return carry

    lax.fori_loop(1, 8, send_final, 0)
    mine_last = s4.at[pl.ds(pl.multiple_of(48 * r, 16), 48)]

    @pl.when(final_date == d)
    def _():
        pltpu.make_async_copy(mine_last, r4.at[z_slot], grad_sem.at[19]).start()

    @pl.when(final_date != d)
    def _():
        remote(
            mine_last, r4.at[z_slot], grad_sem.at[18], grad_sem.at[19], (final_date, r)
        ).start()

    wait_bytes(sa.at[pl.ds(0, 63)], sem.at[0])
    wait_bytes(rs.at[pl.ds(0, 63)], sem.at[2])
    wait_bytes(sc.at[pl.ds(0, 30)], sem.at[4])
    wait_bytes(sb.at[0], sem.at[6])
    wait_bytes(sb.at[1, pl.ds(0, 30)], sem.at[6])

    @pl.when(jnp.logical_not(home))
    def _():
        wait_bytes(sb.at[0, pl.ds(0, 2)], sem.at[6])

    wait_bytes(send_c.at[pl.ds(0, 3)], sem.at[8])
    wait_bytes(send_c.at[3, pl.ds(0, 6)], sem.at[8])
    for chunk, _, _, first_axis, sent, received, second_axis, sent_next, received_next in plans:
        wait_bytes(s1.at[chunk], grad_sem.at[chunk])
        wait_bytes(received, grad_sem.at[6 + chunk])
        wait_bytes(received_next, grad_sem.at[12 + chunk])
    wait_bytes(recv_c, sem.at[9])
    wait_bytes(r4, grad_sem.at[19])
    wait_bytes(r4.at[pl.ds(0, 7)], grad_sem.at[18])

    @pl.when(final_date != d)
    def _():
        wait_bytes(r4.at[0], grad_sem.at[18])


def finish_kernel(recv_c, r4, mixed_ref, project_grad_ref, output_grad_ref):
    small = iota((256, 1), 0)
    order = one_hot((small & 15) * 16 + (small >> 4), 256)
    for when in range(2):
        mixed_ref[256 * when : 256 * when + 256] = matmul(
            order, recv_c[when].reshape(256, D)
        ).astype(bf16)
    total = r4[0].astype(f32)
    for index in range(1, 8):
        total = total + r4[index].astype(f32)
    project_grad_ref[...] = total[:, 0:18]
    output_grad_ref[...] = total[:, 18:24]


VM = pl.BlockSpec(memory_space=pltpu.VMEM)
HB = pl.BlockSpec(memory_space=pltpu.HBM)


def body(
    tokens, clear_flags, date_numbers, decay_slopes, time_project, time_output,
    column_project, column_output, cotangent,
):
    vmem = pltpu.VMEM
    recv_c, r4 = pl.pallas_call(
        layer_kernel,
        out_shape=(
            jax.ShapeDtypeStruct((2, 16, 16, D), bf16),
            jax.ShapeDtypeStruct((8, 48, 128), bf16),
        ),
        in_specs=[HB] * 9,
        out_specs=(VM, VM),
        scratch_shapes=[
            vmem((512, D), bf16),
            vmem((512, D), bf16),
            vmem((32, 16), jnp.int32),
            vmem((D, 3 * D), bf16),
            vmem((D, D), bf16),
            vmem((D, 3 * D), bf16),
            vmem((D, D), bf16),
            pltpu.SMEM((2,), jnp.int32),
            pltpu.SMEM((HEADS,), f32),
            vmem((64, 8, D), bf16),
            vmem((64, 8, D), bf16),
            vmem((16, 1, 128), f32),
            vmem((64, 1, 128), f32),
            vmem((32, 16, D), bf16),
            vmem((2, 32, 8, D), bf16),
            vmem((64, 8, D), bf16),
            vmem((4, 128, D), bf16),
            vmem((64, 128), f32),
            vmem((128, 128), f32),
            vmem((8, 128), f32),
            vmem((512, D), bf16),
            vmem((512, 3 * D), bf16),
            vmem((512, D), bf16),
            vmem((512, D), bf16),
            vmem((512, D), bf16),
            vmem((512, D), bf16),
            vmem((512, 3 * D), bf16),
            vmem((4, 8, 16, D), bf16),
            vmem((1536, D), f32),
            vmem((64, 24, 256), f32),
            vmem((64, 24, 128), f32),
            vmem((3, 768, 128), bf16),
            vmem((3, 768, 128), bf16),
            vmem((2, 4, 192, 128), bf16),
            vmem((2, 3, 192, 128), bf16),
            vmem((2, 8, 24, 128), bf16),
            vmem((2, 7, 24, 128), bf16),
            vmem((8, 96, 128), bf16),
            vmem((7, 96, 128), bf16),
            vmem((4, 24, 128), bf16),
            vmem((3, 24, 128), bf16),
            vmem((D, 128), bf16),
            pltpu.SemaphoreType.DMA((10,)),
            pltpu.SemaphoreType.DMA((20,)),
            pltpu.SemaphoreType.DMA((9,)),
        ],
        compiler_params=pltpu.CompilerParams(
            collective_id=0, has_side_effects=True, vmem_limit_bytes=48 * 1024 * 1024
        ),
        name="layer",
    )(
        tokens.reshape(512, D), cotangent.reshape(512, D), clear_flags.reshape(32, 16),
        time_project, time_output, column_project, column_output, date_numbers, decay_slopes,
    )
    mixed, project_grad, output_grad = pl.pallas_call(
        finish_kernel,
        out_shape=(
            jax.ShapeDtypeStruct((512, D), bf16),
            jax.ShapeDtypeStruct((48, 18), f32),
            jax.ShapeDtypeStruct((48, 6), f32),
        ),
        in_specs=[VM] * 2,
        out_specs=(VM, VM, VM),
        name="finish",
    )(recv_c, r4)
    return mixed.reshape(tokens.shape), project_grad, output_grad


def solution(mesh):
    return jax.shard_map(
        body,
        mesh=mesh,
        in_specs=(
            P("date", "row", None, None), P("date", "row", None), P("date"),
            P(), P(), P(), P(), P(), P("date", "row", None, None),
        ),
        out_specs=(P("date", "row", None, None), P("row", "date"), P("row", "date")),
        check_vma=False,
    )
```

```python
import functools
import math

import jax
import jax.numpy as jnp
from jax import lax
from jax.experimental import pallas as pl
from jax.experimental.pallas import tpu as pltpu
from jax.sharding import PartitionSpec as P

MESH = pl.DeviceIdType.MESH
epsilon = 1e-06
masked_score = -1e30
D = 384
HEADS = 12
GROUPS = 3
inverse_root = 1.0 / math.sqrt(D // HEADS)
bf16, f32 = jnp.bfloat16, jnp.float32


def iota(shape, axis):
    return lax.broadcasted_iota(jnp.int32, shape, axis)


def one_hot(source, width):
    lanes = iota((source.shape[0], width), 1)
    return jnp.where(lanes == source, 1.0, 0.0).astype(bf16)


def matmul(left, right):
    return jnp.dot(left, right, preferred_element_type=f32)


def contract_rows(left, right):
    return lax.dot_general(left, right, (((0,), (0,)), ((), ())), preferred_element_type=f32)


def contract_last(left, right):
    return lax.dot_general(left, right, (((1,), (1,)), ((), ())), preferred_element_type=f32)


def rms_norm(values):
    widened = values.astype(f32)
    factor = lax.rsqrt(jnp.mean(widened * widened, axis=-1, keepdims=True) + epsilon)
    return (widened * factor).astype(bf16)


def head_masks():
    lanes = iota((128, 128), 1) >> 5
    return [lanes == head for head in range(4)]


def stacked(block, masks):
    return jnp.concatenate([jnp.where(mask, block, jnp.zeros_like(block)) for mask in masks], axis=0)


def unstacked(blocks, masks):
    total = jnp.where(masks[0], blocks[0:128], 0.0)
    for head in range(1, 4):
        total = jnp.where(masks[head], blocks[128 * head : 128 * head + 128], total)
    return total


def softmax_block(scores):
    raised = jnp.exp(scores - jnp.max(scores, axis=-1, keepdims=True))
    return raised * (1.0 / jnp.sum(raised, axis=-1, keepdims=True))


def signal(device):
    pl.semaphore_signal(
        pltpu.get_barrier_semaphore(), inc=1, device_id=device, device_id_type=MESH
    )


def remote(source, target, send_sem, recv_sem, device):
    return pltpu.make_async_remote_copy(
        src_ref=source,
        dst_ref=target,
        send_sem=send_sem,
        recv_sem=recv_sem,
        device_id=device,
        device_id_type=MESH,
    )


def wait_bytes(ref, sem):
    pltpu.make_async_copy(ref, ref, sem).wait()


def swing(step, count):
    half = (step + 1) // 2
    return jnp.where(step % 2 == 1, half, count - half)


def layer_kernel(
    tokens_hbm, cotangent_hbm, flags_hbm, time_project_hbm, time_output_hbm,
    column_project_hbm, column_output_hbm, numbers_hbm, slopes_hbm,
    recv_c, r4,
    tokens_ref, rc_in, flags_ref, project_ref, output_ref, column_project_ref, column_output_ref,
    numbers_ref, slopes_ref,
    sa, ra, ss, rs, sc, sb, rb_ref, rc_ref, side, gap_ref, info_ref, base, qkv, heads,
    plane, normed, heads_grad, qkv_grad, send_c, natural, partial_x, partial_y,
    s1, r1, s2x, r2x, s3x, r3x, s2y, r2y, s3y, r3y, s4,
    sem, grad_sem, load_sem,
):
    d, r = lax.axis_index("date"), lax.axis_index("row")
    parity, octet, kk = d % 2, d // 8, (d // 2) % 4
    x, z_lo, core = d % 4, (d // 4) % 2, r % 2
    own = parity * 8 + r
    partner = (d, r + 1 - 2 * core)

    loads = [
        pltpu.make_async_copy(source, target, load_sem.at[index])
        for index, (source, target) in enumerate((
            (tokens_hbm, tokens_ref), (flags_hbm, flags_ref), (numbers_hbm, numbers_ref),
            (cotangent_hbm, rc_in), (time_project_hbm, project_ref), (slopes_hbm, slopes_ref),
            (time_output_hbm, output_ref), (column_output_hbm, column_output_ref),
            (column_project_hbm, column_project_ref),
        ))
    ]
    for load in loads:
        load.start()

    def greet_same_row(step, carry):
        signal(((d + step) % 64, r))
        return carry

    def greet_targets(step, carry):
        signal((2 * step + parity, octet))
        signal((8 * r + 2 * (step // 8) + parity, step % 8))
        return carry

    def greet_columns(step, carry):
        to = (own + step) % 16
        signal((d - parity + to // 8, to % 8))
        return carry

    lax.fori_loop(1, 64, greet_same_row, 0)
    lax.fori_loop(0, 32, greet_targets, 0)
    lax.fori_loop(1, 16, greet_columns, 0)
    signal(partner)
    for index in range(8):
        signal((d - 4 * z_lo + 4 * core, index))
        signal((d - 4 * z_lo + 4 * (index % 2), index - index % 2 + z_lo))

    row = iota((512, 1), 0)
    loads[0].wait()
    target = row >> 3
    column = (target & 1) * 8 + (target >> 3)
    source = ((row >> 2) & 1) * 256 + (((target >> 1) & 3) * 4 + (row & 3)) * 16 + column
    sa[...] = matmul(one_hot(source, 512), tokens_ref[...]).astype(bf16).reshape(64, 8, D)
    loads[1].wait()
    flipped = contract_rows(
        flags_ref[...].astype(f32).astype(bf16), one_hot(iota((32, 1), 0), 128)
    )
    loads[2].wait()
    lane = iota((1, 128), 1)
    first, second = numbers_ref[0], numbers_ref[1]
    extra = jnp.where(lane == 32, first // 32, 0) + jnp.where(lane == 33, second // 32, 0)
    extra = extra + jnp.where(lane == 34, first % 32, 0) + jnp.where(lane == 35, second % 32, 0)
    flipped = flipped + extra.astype(f32)
    for index in range(16):
        ss[index] = flipped[index : index + 1]

    pl.semaphore_wait(pltpu.get_barrier_semaphore(), 63 + 64 + 15 + 1 + 16)

    def send_tokens(step, carry):
        to = (d + swing(step, 64)) % 64
        remote(sa.at[to], ra.at[d], sem.at[0], sem.at[1], (to, r)).start()
        return carry

    def send_side(step, carry):
        to = (d + swing(step, 64)) % 64
        side_of = (to % 2) * 8 + to // 8
        remote(ss.at[side_of], rs.at[d], sem.at[2], sem.at[3], (to, r)).start()
        return carry

    def send_cotangent(step, carry):
        to = (own + step) % 16
        for when in range(2):
            remote(
                sc.at[2 * to + when],
                rc_ref.at[2 * parity + when, pl.ds(pl.multiple_of(16 * r, 16), 16)],
                sem.at[4], sem.at[5], (d - parity + to // 8, to % 8),
            ).start()
        return carry

    lax.fori_loop(1, 64, send_tokens, 0)
    pltpu.make_async_copy(sa.at[d], ra.at[d], sem.at[1]).start()
    lax.fori_loop(1, 64, send_side, 0)
    pltpu.make_async_copy(ss.at[parity * 8 + octet], rs.at[d], sem.at[3]).start()
    loads[3].wait()
    source = ((row >> 4) & 1) * 256 + (row & 15) * 16 + (row >> 5)
    sc[...] = matmul(one_hot(source, 512), rc_in[...]).astype(bf16).reshape(32, 16, D)
    lax.fori_loop(1, 16, send_cotangent, 0)
    for when in range(2):
        pltpu.make_async_copy(
            sc.at[2 * own + when],
            rc_ref.at[2 * parity + when, pl.ds(pl.multiple_of(16 * r, 16), 16)],
            sem.at[5],
        ).start()
    for load in loads[4:]:
        load.wait()

    wait_bytes(ra, sem.at[1])
    source = ((row & 127) >> 1) * 8 + (row & 1) * 4 + (row >> 7)
    ordered = matmul(one_hot(source, 512), ra[...].reshape(512, D)).astype(bf16)
    base[...] = ordered
    qkv[...] = matmul(rms_norm(ordered), project_ref[...]).astype(bf16)

    wait_bytes(rs, sem.at[3])
    for index in range(64):
        side[index : index + 1] = rs[index]
    side_low = side[...].astype(bf16)
    info = jnp.zeros((8, 128), f32)
    pick_row, pick_lane = iota((8, 128), 0), iota((8, 128), 1)
    for when in range(2):
        wanted = jnp.where(pick_row < 4, when * 16 + 4 * kk + pick_row, 32 + when + 2 * (pick_row - 4))
        picked = contract_last(jnp.where(pick_lane == wanted, 1.0, 0.0).astype(bf16), side_low)
        spread = jnp.where(iota((64, 128), 1) == 2 * iota((64, 128), 0) + when, 1.0, 0.0).astype(bf16)
        info = info + matmul(picked.astype(bf16), spread)
    info_ref[...] = info
    days = info[4:5] * 32.0 + info[5:6]
    same_date = iota((128, 128), 0) == iota((128, 128), 1)
    days_down = jnp.sum(jnp.where(same_date, days, 0.0), axis=1, keepdims=True)
    gap_ref[...] = jnp.abs(days_down - days)

    def time_patch(patch, carry):
        rows = pl.ds(pl.multiple_of(patch * 128, 128), 128)
        masks = head_masks()
        allowed = (info_ref[pl.ds(patch, 1), :] > 0.5) | (iota((128, 128), 0) == iota((128, 128), 1))
        for group in range(GROUPS):
            queries = qkv[rows, 128 * group : 128 * group + 128]
            keys = stacked(qkv[rows, D + 128 * group : D + 128 * group + 128], masks)
            values = stacked(qkv[rows, 2 * D + 128 * group : 2 * D + 128 * group + 128], masks)
            scores = contract_last(queries, keys)
            weights = []
            for head in range(4):
                block = scores[:, 128 * head : 128 * head + 128] * inverse_root
                block = block + (-slopes_ref[4 * group + head]) * gap_ref[...]
                block = jnp.where(allowed, block, masked_score)
                weights.append(softmax_block(block).astype(bf16))
            heads[rows, 128 * group : 128 * group + 128] = matmul(
                jnp.concatenate(weights, axis=1), values
            ).astype(bf16)
        return carry

    slot = 2 * (4 * r + kk)
    home = r == octet

    def time_half(half, carry):
        lax.fori_loop(2 * half, 2 * half + 2, time_patch, 0)
        rows = pl.ds(pl.multiple_of(half * 256, 256), 256)
        hidden = (base[rows, :].astype(f32) + matmul(heads[rows, :], output_ref[...])).astype(bf16)
        small = iota((256, 1), 0)
        source = ((small >> 2) & 1) * 128 + (small >> 3) * 4 + (small & 3)
        sb[half] = matmul(one_hot(source, 256), hidden).astype(bf16).reshape(32, 8, D)

        def send_hidden(step, inner):
            to = (d // 2 + swing(step, 32)) % 32
            remote(
                sb.at[half, to], rb_ref.at[slot + half], sem.at[6], sem.at[7],
                (2 * to + parity, octet),
            ).start()
            return inner

        lax.fori_loop(1, 32, send_hidden, 0)

        @pl.when(home)
        def _():
            pltpu.make_async_copy(sb.at[half, d // 2], rb_ref.at[slot + half], sem.at[7]).start()

        @pl.when(jnp.logical_not(home))
        def _():
            remote(
                sb.at[half, d // 2], rb_ref.at[slot + half], sem.at[6], sem.at[7], (d, octet)
            ).start()

        return carry

    lax.fori_loop(0, 2, time_half, 0)

    wait_bytes(rc_ref, sem.at[5])
    heads_grad[...] = contract_last(rc_ref[...].reshape(512, D), column_output_ref[...]).astype(bf16)
    wait_bytes(rb_ref, sem.at[7])

    source = ((row & 127) >> 2) * 16 + (row & 3) * 4 + (row >> 7)
    hidden = matmul(one_hot(source, 512), rb_ref[...].reshape(512, D)).astype(bf16)
    plane[...] = hidden
    column_normed = rms_norm(hidden)
    normed[...] = column_normed
    qkv[...] = matmul(column_normed, column_project_ref[...]).astype(bf16)

    def column_date(date, carry):
        rows = pl.ds(pl.multiple_of(date * 128, 128), 128)
        masks = head_masks()
        for group in range(GROUPS):
            lanes = slice(128 * group, 128 * group + 128)
            queries = qkv[rows, 128 * group : 128 * group + 128]
            keys = stacked(qkv[rows, D + 128 * group : D + 128 * group + 128], masks)
            values = stacked(qkv[rows, 2 * D + 128 * group : 2 * D + 128 * group + 128], masks)
            outer = heads_grad[rows, lanes]
            scores = contract_last(queries, keys)
            products = contract_last(outer, values)
            weights_low, scores_low = [], []
            for head in range(4):
                weights = softmax_block(scores[:, 128 * head : 128 * head + 128] * inverse_root)
                product = products[:, 128 * head : 128 * head + 128]
                centre = jnp.sum(weights * product, axis=-1, keepdims=True)
                weights_low.append(weights.astype(bf16))
                scores_low.append((weights * (product - centre)).astype(bf16))
            low = jnp.concatenate(weights_low, axis=1)
            score_low = jnp.concatenate(scores_low, axis=1)
            heads[rows, lanes] = matmul(low, values).astype(bf16)
            qkv_grad[rows, 128 * group : 128 * group + 128] = (
                matmul(score_low, keys) * inverse_root
            ).astype(bf16)
            qkv_grad[rows, D + 128 * group : D + 128 * group + 128] = (
                unstacked(contract_rows(score_low, queries), masks) * inverse_root
            ).astype(bf16)
            qkv_grad[rows, 2 * D + 128 * group : 2 * D + 128 * group + 128] = unstacked(
                contract_rows(low, outer), masks
            ).astype(bf16)
        mixed = plane[rows, :].astype(f32) + matmul(heads[rows, :], column_output_ref[...])
        send_c[date] = mixed.astype(bf16).reshape(8, 16, D)
        to_date = d - parity + date // 2

        def send_rows(step, inner):
            to = (r + swing(step, 8)) % 8
            remote(
                send_c.at[date, to], recv_c.at[date % 2, own], sem.at[8], sem.at[9], (to_date, to)
            ).start()
            return inner

        lax.fori_loop(1, 8, send_rows, 0)

        @pl.when(to_date == d)
        def _():
            pltpu.make_async_copy(send_c.at[date, r], recv_c.at[date % 2, own], sem.at[9]).start()

        @pl.when(to_date != d)
        def _():
            remote(
                send_c.at[date, r], recv_c.at[date % 2, own], sem.at[8], sem.at[9], (to_date, r)
            ).start()

        return carry

    lax.fori_loop(0, 4, column_date, 0)

    natural[0:1152] = contract_rows(qkv_grad[...], normed[...])
    natural[1152:1536] = contract_rows(rc_ref[...].reshape(512, D), heads[...])
    for block in range(64):
        bits = (block % 8) * 8 + (block // 32) * 4 + (block // 8) % 4
        flipped_block = (block // 32) * 32 + (block % 8) * 4 + (block // 8) % 4
        partial_y[flipped_block, 0:18] = natural[18 * bits : 18 * bits + 18, 256:384]
        partial_y[flipped_block, 18:24] = natural[1152 + 6 * bits : 1152 + 6 * bits + 6, 256:384]
        partial_x[block, 0:18] = natural[18 * bits : 18 * bits + 18, 0:256]
        partial_x[block, 18:24] = natural[1152 + 6 * bits : 1152 + 6 * bits + 6, 0:256]

    along_x = (x, 4, 1, (1, 3, 2), lambda step: (d - x + (x + step) % 4, r))
    along_y = (octet, 8, 8, (1, 7, 2, 6, 3, 5, 4), lambda step: ((d + 8 * step) % 64, r))
    plans = (
        (2, partial_y, 0, along_y, s2y, r2y, along_x, s3y, r3y),
        (0, partial_x, 0, along_x, s2x.at[0], r2x.at[0], along_y, s3x.at[0], r3x.at[0]),
        (1, partial_x, 128, along_x, s2x.at[1], r2x.at[1], along_y, s3x.at[1], r3x.at[1]),
    )

    def exchange(axis, sent, received, send_sem, recv_sem):
        me, size, _, steps, device = axis
        for step in steps:
            remote(
                sent.at[(me + step) % size], received.at[step - 1], send_sem, recv_sem, device(step)
            ).start()

    def gathered(axis, sent, received, recv_sem):
        me, size = axis[:2]
        wait_bytes(received, recv_sem)
        total = sent[me].astype(f32)
        for index in range(size - 1):
            total = total + received[index].astype(f32)
        return total

    for chunk, partial, low, *_ in plans:
        other = partial[pl.ds(pl.multiple_of(32 - 32 * core, 32), 32), :, low : low + 128]
        s1[chunk] = other.reshape(768, 128).astype(bf16)
        remote(
            s1.at[chunk], r1.at[chunk], grad_sem.at[chunk], grad_sem.at[3 + chunk], partner
        ).start()
    for chunk, partial, low, first_axis, sent, received, *_ in plans:
        mine = partial[pl.ds(pl.multiple_of(32 * core, 32), 32), :, low : low + 128].reshape(768, 128)
        wait_bytes(r1.at[chunk], grad_sem.at[3 + chunk])
        size = first_axis[1]
        sent[...] = (mine + r1[chunk].astype(f32)).astype(bf16).reshape(size, 768 // size, 128)
        exchange(first_axis, sent, received, grad_sem.at[6 + chunk], grad_sem.at[9 + chunk])
    for chunk, _, _, first_axis, sent, received, second_axis, sent_next, received_next in plans:
        total = gathered(first_axis, sent, received, grad_sem.at[9 + chunk])
        sent_next[...] = total.reshape(second_axis[1], 24, 128).astype(bf16)
        exchange(
            second_axis, sent_next, received_next, grad_sem.at[12 + chunk], grad_sem.at[15 + chunk]
        )
    for chunk, _, _, _, _, _, second_axis, sent_next, received_next in plans:
        total = gathered(second_axis, sent_next, received_next, grad_sem.at[15 + chunk])
        square = jnp.concatenate([total, jnp.zeros((104, 128), f32)], axis=0)
        s4[128 * chunk : 128 * chunk + 128] = jnp.transpose(square).astype(bf16)
    z_slot = (r // 2) * 2 + z_lo
    final_date = d - 4 * z_lo + 4 * core

    def send_final(step, carry):
        to = (r + swing(step, 8)) % 8
        remote(
            s4.at[pl.ds(pl.multiple_of(48 * to, 16), 48)], r4.at[z_slot],
            grad_sem.at[18], grad_sem.at[19], (final_date, to),
        ).start()
        return carry

    lax.fori_loop(1, 8, send_final, 0)
    mine_last = s4.at[pl.ds(pl.multiple_of(48 * r, 16), 48)]

    @pl.when(final_date == d)
    def _():
        pltpu.make_async_copy(mine_last, r4.at[z_slot], grad_sem.at[19]).start()

    @pl.when(final_date != d)
    def _():
        remote(
            mine_last, r4.at[z_slot], grad_sem.at[18], grad_sem.at[19], (final_date, r)
        ).start()

    wait_bytes(sa.at[pl.ds(0, 63)], sem.at[0])
    wait_bytes(rs.at[pl.ds(0, 63)], sem.at[2])
    wait_bytes(sc.at[pl.ds(0, 30)], sem.at[4])
    wait_bytes(sb.at[0], sem.at[6])
    wait_bytes(sb.at[1, pl.ds(0, 30)], sem.at[6])

    @pl.when(jnp.logical_not(home))
    def _():
        wait_bytes(sb.at[0, pl.ds(0, 2)], sem.at[6])

    wait_bytes(send_c.at[pl.ds(0, 3)], sem.at[8])
    wait_bytes(send_c.at[3, pl.ds(0, 6)], sem.at[8])
    for chunk, _, _, first_axis, sent, received, second_axis, sent_next, received_next in plans:
        wait_bytes(s1.at[chunk], grad_sem.at[chunk])
        wait_bytes(received, grad_sem.at[6 + chunk])
        wait_bytes(received_next, grad_sem.at[12 + chunk])
    wait_bytes(recv_c, sem.at[9])
    wait_bytes(r4, grad_sem.at[19])
    wait_bytes(r4.at[pl.ds(0, 7)], grad_sem.at[18])

    @pl.when(final_date != d)
    def _():
        wait_bytes(r4.at[0], grad_sem.at[18])


def finish_kernel(recv_c, r4, mixed_ref, project_grad_ref, output_grad_ref):
    small = iota((256, 1), 0)
    order = one_hot((small & 15) * 16 + (small >> 4), 256)
    for when in range(2):
        mixed_ref[256 * when : 256 * when + 256] = matmul(
            order, recv_c[when].reshape(256, D)
        ).astype(bf16)
    total = r4[0].astype(f32)
    for index in range(1, 8):
        total = total + r4[index].astype(f32)
    turned = jnp.transpose(jnp.concatenate([total, jnp.zeros((80, 128), f32)], axis=0))
    project_grad_ref[...] = turned[0:18, 0:48]
    output_grad_ref[...] = turned[18:24, 0:48]


VM = pl.BlockSpec(memory_space=pltpu.VMEM)
HB = pl.BlockSpec(memory_space=pltpu.HBM)


def body(
    tokens, clear_flags, date_numbers, decay_slopes, time_project, time_output,
    column_project, column_output, cotangent,
):
    vmem = pltpu.VMEM
    recv_c, r4 = pl.pallas_call(
        layer_kernel,
        out_shape=(
            jax.ShapeDtypeStruct((2, 16, 16, D), bf16),
            jax.ShapeDtypeStruct((8, 48, 128), bf16),
        ),
        in_specs=[HB] * 9,
        out_specs=(VM, VM),
        scratch_shapes=[
            vmem((512, D), bf16),
            vmem((512, D), bf16),
            vmem((32, 16), jnp.int32),
            vmem((D, 3 * D), bf16),
            vmem((D, D), bf16),
            vmem((D, 3 * D), bf16),
            vmem((D, D), bf16),
            pltpu.SMEM((2,), jnp.int32),
            pltpu.SMEM((HEADS,), f32),
            vmem((64, 8, D), bf16),
            vmem((64, 8, D), bf16),
            vmem((16, 1, 128), f32),
            vmem((64, 1, 128), f32),
            vmem((32, 16, D), bf16),
            vmem((2, 32, 8, D), bf16),
            vmem((64, 8, D), bf16),
            vmem((4, 128, D), bf16),
            vmem((64, 128), f32),
            vmem((128, 128), f32),
            vmem((8, 128), f32),
            vmem((512, D), bf16),
            vmem((512, 3 * D), bf16),
            vmem((512, D), bf16),
            vmem((512, D), bf16),
            vmem((512, D), bf16),
            vmem((512, D), bf16),
            vmem((512, 3 * D), bf16),
            vmem((4, 8, 16, D), bf16),
            vmem((1536, D), f32),
            vmem((64, 24, 256), f32),
            vmem((64, 24, 128), f32),
            vmem((3, 768, 128), bf16),
            vmem((3, 768, 128), bf16),
            vmem((2, 4, 192, 128), bf16),
            vmem((2, 3, 192, 128), bf16),
            vmem((2, 8, 24, 128), bf16),
            vmem((2, 7, 24, 128), bf16),
            vmem((8, 96, 128), bf16),
            vmem((7, 96, 128), bf16),
            vmem((4, 24, 128), bf16),
            vmem((3, 24, 128), bf16),
            vmem((D, 128), bf16),
            pltpu.SemaphoreType.DMA((10,)),
            pltpu.SemaphoreType.DMA((20,)),
            pltpu.SemaphoreType.DMA((9,)),
        ],
        compiler_params=pltpu.CompilerParams(
            collective_id=0, has_side_effects=True, vmem_limit_bytes=48 * 1024 * 1024
        ),
        name="layer",
    )(
        *(
            pltpu.with_memory_space_constraint(value, pltpu.HBM)
            for value in (
                tokens.reshape(512, D), cotangent.reshape(512, D), clear_flags.reshape(32, 16),
                time_project, time_output, column_project, column_output, date_numbers, decay_slopes,
            )
        )
    )
    mixed, project_grad, output_grad = pl.pallas_call(
        finish_kernel,
        out_shape=(
            jax.ShapeDtypeStruct((512, D), bf16),
            jax.ShapeDtypeStruct((18, 48), f32),
            jax.ShapeDtypeStruct((6, 48), f32),
        ),
        in_specs=[VM] * 2,
        out_specs=(VM, VM, VM),
        compiler_params=pltpu.CompilerParams(vmem_limit_bytes=8 * 1024 * 1024),
        name="finish",
    )(recv_c, r4)
    return mixed.reshape(tokens.shape), project_grad.T, output_grad.T


def solution(mesh):
    return jax.shard_map(
        body,
        mesh=mesh,
        in_specs=(
            P("date", "row", None, None), P("date", "row", None), P("date"),
            P(), P(), P(), P(), P(), P("date", "row", None, None),
        ),
        out_specs=(P("date", "row", None, None), P("row", "date"), P("row", "date")),
        check_vma=False,
    )
```

```python
import functools
import math

import jax
import jax.numpy as jnp
from jax import lax
from jax.experimental import pallas as pl
from jax.experimental.pallas import tpu as pltpu
from jax.sharding import PartitionSpec as P

MESH = pl.DeviceIdType.MESH
epsilon = 1e-06
masked_score = -1e30
D = 384
HEADS = 12
GROUPS = 3
inverse_root = 1.0 / math.sqrt(D // HEADS)
bf16, f32 = jnp.bfloat16, jnp.float32


def iota(shape, axis):
    return lax.broadcasted_iota(jnp.int32, shape, axis)


def one_hot(source, width):
    lanes = iota((source.shape[0], width), 1)
    return jnp.where(lanes == source, 1.0, 0.0).astype(bf16)


def matmul(left, right):
    return jnp.dot(left, right, preferred_element_type=f32)


def contract_rows(left, right):
    return lax.dot_general(left, right, (((0,), (0,)), ((), ())), preferred_element_type=f32)


def contract_last(left, right):
    return lax.dot_general(left, right, (((1,), (1,)), ((), ())), preferred_element_type=f32)


def rms_norm(values):
    widened = values.astype(f32)
    factor = lax.rsqrt(jnp.mean(widened * widened, axis=-1, keepdims=True) + epsilon)
    return (widened * factor).astype(bf16)


def head_masks():
    lanes = iota((128, 128), 1) >> 5
    return [lanes == head for head in range(4)]


def stacked(block, masks):
    return jnp.concatenate([jnp.where(mask, block, jnp.zeros_like(block)) for mask in masks], axis=0)


def unstacked(blocks, masks):
    total = jnp.where(masks[0], blocks[0:128], 0.0)
    for head in range(1, 4):
        total = jnp.where(masks[head], blocks[128 * head : 128 * head + 128], total)
    return total


def softmax_block(scores):
    raised = jnp.exp(scores - jnp.max(scores, axis=-1, keepdims=True))
    return raised * (1.0 / jnp.sum(raised, axis=-1, keepdims=True))


def signal(device):
    pl.semaphore_signal(
        pltpu.get_barrier_semaphore(), inc=1, device_id=device, device_id_type=MESH
    )


def remote(source, target, send_sem, recv_sem, device):
    return pltpu.make_async_remote_copy(
        src_ref=source,
        dst_ref=target,
        send_sem=send_sem,
        recv_sem=recv_sem,
        device_id=device,
        device_id_type=MESH,
    )


def wait_bytes(ref, sem):
    pltpu.make_async_copy(ref, ref, sem).wait()


def swing(step, count):
    half = (step + 1) // 2
    return jnp.where(step % 2 == 1, half, count - half)


def layer_kernel(
    tokens_hbm, cotangent_hbm, flags_hbm, time_project_hbm, time_output_hbm,
    column_project_hbm, column_output_hbm, numbers_hbm, slopes_hbm,
    recv_c, r4,
    tokens_ref, rc_in, flags_ref, project_ref, output_ref, column_project_ref, column_output_ref,
    numbers_ref, slopes_ref,
    sa, ra, ss, rs, sc, sb, rb_ref, rc_ref, side, gap_ref, info_ref, base, qkv, heads,
    plane, normed, heads_grad, qkv_grad, send_c, natural, partial_x, partial_y,
    s1, r1, s2x, r2x, s3x, r3x, s2y, r2y, s3y, r3y, s4,
    sem, grad_sem, load_sem, b_sem,
):
    d, r = lax.axis_index("date"), lax.axis_index("row")
    parity, octet, kk = d % 2, d // 8, (d // 2) % 4
    x, z_lo, core = d % 4, (d // 4) % 2, r % 2
    own = parity * 8 + r
    partner = (d, r + 1 - 2 * core)

    loads = [
        pltpu.make_async_copy(source, target, load_sem.at[index])
        for index, (source, target) in enumerate((
            (tokens_hbm, tokens_ref), (flags_hbm, flags_ref), (numbers_hbm, numbers_ref),
            (cotangent_hbm, rc_in), (time_project_hbm, project_ref), (slopes_hbm, slopes_ref),
            (time_output_hbm, output_ref), (column_output_hbm, column_output_ref),
            (column_project_hbm, column_project_ref),
        ))
    ]
    for load in loads:
        load.start()

    def greet_same_row(step, carry):
        signal(((d + step) % 64, r))
        return carry

    def greet_targets(step, carry):
        signal((2 * step + parity, octet))
        signal((8 * r + 2 * (step // 8) + parity, step % 8))
        return carry

    def greet_columns(step, carry):
        to = (own + step) % 16
        signal((d - parity + to // 8, to % 8))
        return carry

    lax.fori_loop(1, 64, greet_same_row, 0)
    lax.fori_loop(0, 32, greet_targets, 0)
    lax.fori_loop(1, 16, greet_columns, 0)
    signal(partner)
    for index in range(8):
        signal((d - 4 * z_lo + 4 * core, index))
        signal((d - 4 * z_lo + 4 * (index % 2), index - index % 2 + z_lo))

    row = iota((512, 1), 0)
    loads[0].wait()
    target = row >> 3
    column = (target & 1) * 8 + (target >> 3)
    source = ((row >> 2) & 1) * 256 + (((target >> 1) & 3) * 4 + (row & 3)) * 16 + column
    sa[...] = matmul(one_hot(source, 512), tokens_ref[...]).astype(bf16).reshape(64, 8, D)
    loads[1].wait()
    flipped = contract_rows(
        flags_ref[...].astype(f32).astype(bf16), one_hot(iota((32, 1), 0), 128)
    )
    loads[2].wait()
    lane = iota((1, 128), 1)
    first, second = numbers_ref[0], numbers_ref[1]
    extra = jnp.where(lane == 32, first // 32, 0) + jnp.where(lane == 33, second // 32, 0)
    extra = extra + jnp.where(lane == 34, first % 32, 0) + jnp.where(lane == 35, second % 32, 0)
    flipped = flipped + extra.astype(f32)
    for index in range(16):
        ss[index] = flipped[index : index + 1]

    pl.semaphore_wait(pltpu.get_barrier_semaphore(), 63 + 64 + 15 + 1 + 16)

    def send_tokens(step, carry):
        to = (d + swing(step, 64)) % 64
        remote(sa.at[to], ra.at[d], sem.at[0], sem.at[1], (to, r)).start()
        return carry

    def send_side(step, carry):
        to = (d + swing(step, 64)) % 64
        side_of = (to % 2) * 8 + to // 8
        remote(ss.at[side_of], rs.at[d], sem.at[2], sem.at[3], (to, r)).start()
        return carry

    def send_cotangent(step, carry):
        to = (own + step) % 16
        for when in range(2):
            remote(
                sc.at[2 * to + when],
                rc_ref.at[2 * parity + when, pl.ds(pl.multiple_of(16 * r, 16), 16)],
                sem.at[4], sem.at[5], (d - parity + to // 8, to % 8),
            ).start()
        return carry

    lax.fori_loop(1, 64, send_tokens, 0)
    pltpu.make_async_copy(sa.at[d], ra.at[d], sem.at[1]).start()
    lax.fori_loop(1, 64, send_side, 0)
    pltpu.make_async_copy(ss.at[parity * 8 + octet], rs.at[d], sem.at[3]).start()
    loads[3].wait()
    source = ((row >> 4) & 1) * 256 + (row & 15) * 16 + (row >> 5)
    sc[...] = matmul(one_hot(source, 512), rc_in[...]).astype(bf16).reshape(32, 16, D)
    lax.fori_loop(1, 16, send_cotangent, 0)
    for when in range(2):
        pltpu.make_async_copy(
            sc.at[2 * own + when],
            rc_ref.at[2 * parity + when, pl.ds(pl.multiple_of(16 * r, 16), 16)],
            sem.at[5],
        ).start()
    for load in loads[4:]:
        load.wait()

    wait_bytes(ra, sem.at[1])
    source = (((row >> 1) & 31) * 2 + ((row >> 6) & 1)) * 8 + (row & 1) * 4 + (row >> 7)
    ordered = matmul(one_hot(source, 512), ra[...].reshape(512, D)).astype(bf16)
    for piece in range(8):
        patch, half = piece // 2, piece % 2
        base[half, 64 * patch : 64 * patch + 64] = ordered[64 * piece : 64 * piece + 64]
    qkv[...] = matmul(rms_norm(ordered), project_ref[...]).astype(bf16)

    wait_bytes(rs, sem.at[3])
    for index in range(64):
        side[index : index + 1] = rs[index]
    side_low = side[...].astype(bf16)
    info = jnp.zeros((8, 128), f32)
    pick_row, pick_lane = iota((8, 128), 0), iota((8, 128), 1)
    for when in range(2):
        wanted = jnp.where(pick_row < 4, when * 16 + 4 * kk + pick_row, 32 + when + 2 * (pick_row - 4))
        picked = contract_last(jnp.where(pick_lane == wanted, 1.0, 0.0).astype(bf16), side_low)
        giver = iota((64, 128), 0)
        place = (giver & 1) * 64 + (giver >> 1) * 2 + when
        spread = jnp.where(iota((64, 128), 1) == place, 1.0, 0.0).astype(bf16)
        info = info + matmul(picked.astype(bf16), spread)
    info_ref[...] = info
    days = info[4:5] * 32.0 + info[5:6]
    same_date = iota((128, 128), 0) == iota((128, 128), 1)
    days_down = jnp.sum(jnp.where(same_date, days, 0.0), axis=1, keepdims=True)
    gap_ref[...] = jnp.abs(days_down - days)

    def time_patch(half, patch):
        rows = pl.ds(pl.multiple_of(patch * 128 + half * 64, 64), 64)
        keys_rows = pl.ds(pl.multiple_of(patch * 128, 128), 128)
        out_rows = pl.ds(pl.multiple_of(patch * 64, 64), 64)
        masks = head_masks()
        allowed = (info_ref[pl.ds(patch, 1), :] > 0.5) | (
            iota((64, 128), 0) + 64 * half == iota((64, 128), 1)
        )
        gap = gap_ref[pl.ds(pl.multiple_of(half * 64, 64), 64), :]
        for group in range(GROUPS):
            queries = qkv[rows, 128 * group : 128 * group + 128]
            keys = stacked(qkv[keys_rows, D + 128 * group : D + 128 * group + 128], masks)
            values = stacked(qkv[keys_rows, 2 * D + 128 * group : 2 * D + 128 * group + 128], masks)
            scores = contract_last(queries, keys)
            weights = []
            for head in range(4):
                block = scores[:, 128 * head : 128 * head + 128] * inverse_root
                block = block + (-slopes_ref[4 * group + head]) * gap
                block = jnp.where(allowed, block, masked_score)
                weights.append(softmax_block(block).astype(bf16))
            heads[out_rows, 128 * group : 128 * group + 128] = matmul(
                jnp.concatenate(weights, axis=1), values
            ).astype(bf16)

    slot = 4 * r + kk
    home = r == octet

    def time_half(half, carry):
        def time_pair(pair, inner):
            time_patch(half, 2 * pair)
            time_patch(half, 2 * pair + 1)
            return inner

        lax.fori_loop(0, 2, time_pair, 0)
        hidden = (
            base[half].astype(f32) + matmul(heads[0:256, :], output_ref[...])
        ).astype(bf16)
        small = iota((256, 1), 0)
        source = ((small >> 1) & 3) * 64 + (small >> 3) * 2 + (small & 1)
        sb[half] = matmul(one_hot(source, 256), hidden).astype(bf16).reshape(32, 8, D)

        def send_hidden(step, inner):
            to = (d // 2 + swing(step, 32)) % 32
            remote(
                sb.at[half, to], rb_ref.at[half, slot], b_sem.at[half], b_sem.at[2 + half],
                (2 * to + parity, octet),
            ).start()
            return inner

        lax.fori_loop(1, 32, send_hidden, 0)

        @pl.when(home)
        def _():
            pltpu.make_async_copy(sb.at[half, d // 2], rb_ref.at[half, slot], b_sem.at[2 + half]).start()

        @pl.when(jnp.logical_not(home))
        def _():
            remote(
                sb.at[half, d // 2], rb_ref.at[half, slot], b_sem.at[half], b_sem.at[2 + half], (d, octet)
            ).start()

        return carry

    lax.fori_loop(0, 2, time_half, 0)

    wait_bytes(rc_ref, sem.at[5])
    heads_grad[...] = contract_last(rc_ref[...].reshape(512, D), column_output_ref[...]).astype(bf16)
    def column_date(date, carry):
        rows = pl.ds(pl.multiple_of(date * 128, 128), 128)
        masks = head_masks()
        for group in range(GROUPS):
            lanes = slice(128 * group, 128 * group + 128)
            queries = qkv[rows, 128 * group : 128 * group + 128]
            keys = stacked(qkv[rows, D + 128 * group : D + 128 * group + 128], masks)
            values = stacked(qkv[rows, 2 * D + 128 * group : 2 * D + 128 * group + 128], masks)
            outer = heads_grad[rows, lanes]
            scores = contract_last(queries, keys)
            products = contract_last(outer, values)
            weights_low, scores_low = [], []
            for head in range(4):
                weights = softmax_block(scores[:, 128 * head : 128 * head + 128] * inverse_root)
                product = products[:, 128 * head : 128 * head + 128]
                centre = jnp.sum(weights * product, axis=-1, keepdims=True)
                weights_low.append(weights.astype(bf16))
                scores_low.append((weights * (product - centre)).astype(bf16))
            low = jnp.concatenate(weights_low, axis=1)
            score_low = jnp.concatenate(scores_low, axis=1)
            heads[rows, lanes] = matmul(low, values).astype(bf16)
            qkv_grad[rows, 128 * group : 128 * group + 128] = (
                matmul(score_low, keys) * inverse_root
            ).astype(bf16)
            qkv_grad[rows, D + 128 * group : D + 128 * group + 128] = (
                unstacked(contract_rows(score_low, queries), masks) * inverse_root
            ).astype(bf16)
            qkv_grad[rows, 2 * D + 128 * group : 2 * D + 128 * group + 128] = unstacked(
                contract_rows(low, outer), masks
            ).astype(bf16)
        mixed = plane[rows, :].astype(f32) + matmul(heads[rows, :], column_output_ref[...])
        send_c[date] = mixed.astype(bf16).reshape(8, 16, D)
        to_date = d - parity + date // 2

        def send_rows(step, inner):
            to = (r + swing(step, 8)) % 8
            remote(
                send_c.at[date, to], recv_c.at[date % 2, own], sem.at[8], sem.at[9], (to_date, to)
            ).start()
            return inner

        lax.fori_loop(1, 8, send_rows, 0)

        @pl.when(to_date == d)
        def _():
            pltpu.make_async_copy(send_c.at[date, r], recv_c.at[date % 2, own], sem.at[9]).start()

        @pl.when(to_date != d)
        def _():
            remote(
                send_c.at[date, r], recv_c.at[date % 2, own], sem.at[8], sem.at[9], (to_date, r)
            ).start()

        return carry

    def column_half(half, carry):
        wait_bytes(rb_ref.at[half], b_sem.at[2 + half])
        rows = pl.ds(pl.multiple_of(half * 256, 256), 256)
        small = iota((256, 1), 0)
        source = (small & 127) * 2 + (small >> 7)
        hidden = matmul(one_hot(source, 256), rb_ref[half].reshape(256, D)).astype(bf16)
        plane[rows, :] = hidden
        column_normed = rms_norm(hidden)
        normed[rows, :] = column_normed
        qkv[rows, :] = matmul(column_normed, column_project_ref[...]).astype(bf16)
        return lax.fori_loop(2 * half, 2 * half + 2, column_date, carry)

    lax.fori_loop(0, 2, column_half, 0)

    natural[0:1152] = contract_rows(qkv_grad[...], normed[...])
    natural[1152:1536] = contract_rows(rc_ref[...].reshape(512, D), heads[...])
    for block in range(64):
        bits = (block % 8) * 8 + (block // 32) * 4 + (block // 8) % 4
        flipped_block = (block // 32) * 32 + (block % 8) * 4 + (block // 8) % 4
        partial_y[flipped_block, 0:18] = natural[18 * bits : 18 * bits + 18, 256:384]
        partial_y[flipped_block, 18:24] = natural[1152 + 6 * bits : 1152 + 6 * bits + 6, 256:384]
        partial_x[block, 0:18] = natural[18 * bits : 18 * bits + 18, 0:256]
        partial_x[block, 18:24] = natural[1152 + 6 * bits : 1152 + 6 * bits + 6, 0:256]

    along_x = (x, 4, 1, (1, 3, 2), lambda step: (d - x + (x + step) % 4, r))
    along_y = (octet, 8, 8, (1, 7, 2, 6, 3, 5, 4), lambda step: ((d + 8 * step) % 64, r))
    plans = (
        (2, partial_y, 0, along_y, s2y, r2y, along_x, s3y, r3y),
        (0, partial_x, 0, along_x, s2x.at[0], r2x.at[0], along_y, s3x.at[0], r3x.at[0]),
        (1, partial_x, 128, along_x, s2x.at[1], r2x.at[1], along_y, s3x.at[1], r3x.at[1]),
    )

    def exchange(axis, sent, received, send_sem, recv_sem):
        me, size, _, steps, device = axis
        for step in steps:
            remote(
                sent.at[(me + step) % size], received.at[step - 1], send_sem, recv_sem, device(step)
            ).start()

    def gathered(axis, sent, received, recv_sem):
        me, size = axis[:2]
        wait_bytes(received, recv_sem)
        total = sent[me].astype(f32)
        for index in range(size - 1):
            total = total + received[index].astype(f32)
        return total

    for chunk, partial, low, *_ in plans:
        other = partial[pl.ds(pl.multiple_of(32 - 32 * core, 32), 32), :, low : low + 128]
        s1[chunk] = other.reshape(768, 128).astype(bf16)
        remote(
            s1.at[chunk], r1.at[chunk], grad_sem.at[chunk], grad_sem.at[3 + chunk], partner
        ).start()
    for chunk, partial, low, first_axis, sent, received, *_ in plans:
        mine = partial[pl.ds(pl.multiple_of(32 * core, 32), 32), :, low : low + 128].reshape(768, 128)
        wait_bytes(r1.at[chunk], grad_sem.at[3 + chunk])
        size = first_axis[1]
        sent[...] = (mine + r1[chunk].astype(f32)).astype(bf16).reshape(size, 768 // size, 128)
        exchange(first_axis, sent, received, grad_sem.at[6 + chunk], grad_sem.at[9 + chunk])
    for chunk, _, _, first_axis, sent, received, second_axis, sent_next, received_next in plans:
        total = gathered(first_axis, sent, received, grad_sem.at[9 + chunk])
        sent_next[...] = total.reshape(second_axis[1], 24, 128).astype(bf16)
        exchange(
            second_axis, sent_next, received_next, grad_sem.at[12 + chunk], grad_sem.at[15 + chunk]
        )
    for chunk, _, _, _, _, _, second_axis, sent_next, received_next in plans:
        total = gathered(second_axis, sent_next, received_next, grad_sem.at[15 + chunk])
        square = jnp.concatenate([total, jnp.zeros((104, 128), f32)], axis=0)
        s4[128 * chunk : 128 * chunk + 128] = jnp.transpose(square).astype(bf16)
    z_slot = (r // 2) * 2 + z_lo
    final_date = d - 4 * z_lo + 4 * core

    def send_final(step, carry):
        to = (r + swing(step, 8)) % 8
        remote(
            s4.at[pl.ds(pl.multiple_of(48 * to, 16), 48)], r4.at[z_slot],
            grad_sem.at[18], grad_sem.at[19], (final_date, to),
        ).start()
        return carry

    lax.fori_loop(1, 8, send_final, 0)
    mine_last = s4.at[pl.ds(pl.multiple_of(48 * r, 16), 48)]

    @pl.when(final_date == d)
    def _():
        pltpu.make_async_copy(mine_last, r4.at[z_slot], grad_sem.at[19]).start()

    @pl.when(final_date != d)
    def _():
        remote(
            mine_last, r4.at[z_slot], grad_sem.at[18], grad_sem.at[19], (final_date, r)
        ).start()

    wait_bytes(sa.at[pl.ds(0, 63)], sem.at[0])
    wait_bytes(rs.at[pl.ds(0, 63)], sem.at[2])
    wait_bytes(sc.at[pl.ds(0, 30)], sem.at[4])
    for half in range(2):
        wait_bytes(sb.at[half, pl.ds(0, 31)], b_sem.at[half])

    @pl.when(jnp.logical_not(home))
    def _():
        for half in range(2):
            wait_bytes(sb.at[half, 0], b_sem.at[half])

    wait_bytes(send_c.at[pl.ds(0, 3)], sem.at[8])
    wait_bytes(send_c.at[3, pl.ds(0, 6)], sem.at[8])
    for chunk, _, _, first_axis, sent, received, second_axis, sent_next, received_next in plans:
        wait_bytes(s1.at[chunk], grad_sem.at[chunk])
        wait_bytes(received, grad_sem.at[6 + chunk])
        wait_bytes(received_next, grad_sem.at[12 + chunk])
    wait_bytes(recv_c, sem.at[9])
    wait_bytes(r4, grad_sem.at[19])
    wait_bytes(r4.at[pl.ds(0, 7)], grad_sem.at[18])

    @pl.when(final_date != d)
    def _():
        wait_bytes(r4.at[0], grad_sem.at[18])


def finish_kernel(recv_c, r4, mixed_ref, project_grad_ref, output_grad_ref):
    small = iota((256, 1), 0)
    order = one_hot((small & 15) * 16 + (small >> 4), 256)
    for when in range(2):
        mixed_ref[256 * when : 256 * when + 256] = matmul(
            order, recv_c[when].reshape(256, D)
        ).astype(bf16)
    total = r4[0].astype(f32)
    for index in range(1, 8):
        total = total + r4[index].astype(f32)
    turned = jnp.transpose(jnp.concatenate([total, jnp.zeros((80, 128), f32)], axis=0))
    project_grad_ref[...] = turned[0:18, 0:48]
    output_grad_ref[...] = turned[18:24, 0:48]


VM = pl.BlockSpec(memory_space=pltpu.VMEM)
HB = pl.BlockSpec(memory_space=pltpu.HBM)


def body(
    tokens, clear_flags, date_numbers, decay_slopes, time_project, time_output,
    column_project, column_output, cotangent,
):
    vmem = pltpu.VMEM
    recv_c, r4 = pl.pallas_call(
        layer_kernel,
        out_shape=(
            jax.ShapeDtypeStruct((2, 16, 16, D), bf16),
            jax.ShapeDtypeStruct((8, 48, 128), bf16),
        ),
        in_specs=[HB] * 9,
        out_specs=(VM, VM),
        scratch_shapes=[
            vmem((512, D), bf16),
            vmem((512, D), bf16),
            vmem((32, 16), jnp.int32),
            vmem((D, 3 * D), bf16),
            vmem((D, D), bf16),
            vmem((D, 3 * D), bf16),
            vmem((D, D), bf16),
            pltpu.SMEM((2,), jnp.int32),
            pltpu.SMEM((HEADS,), f32),
            vmem((64, 8, D), bf16),
            vmem((64, 8, D), bf16),
            vmem((16, 1, 128), f32),
            vmem((64, 1, 128), f32),
            vmem((32, 16, D), bf16),
            vmem((2, 32, 8, D), bf16),
            vmem((2, 32, 8, D), bf16),
            vmem((4, 128, D), bf16),
            vmem((64, 128), f32),
            vmem((128, 128), f32),
            vmem((8, 128), f32),
            vmem((2, 256, D), bf16),
            vmem((512, 3 * D), bf16),
            vmem((512, D), bf16),
            vmem((512, D), bf16),
            vmem((512, D), bf16),
            vmem((512, D), bf16),
            vmem((512, 3 * D), bf16),
            vmem((4, 8, 16, D), bf16),
            vmem((1536, D), f32),
            vmem((64, 24, 256), f32),
            vmem((64, 24, 128), f32),
            vmem((3, 768, 128), bf16),
            vmem((3, 768, 128), bf16),
            vmem((2, 4, 192, 128), bf16),
            vmem((2, 3, 192, 128), bf16),
            vmem((2, 8, 24, 128), bf16),
            vmem((2, 7, 24, 128), bf16),
            vmem((8, 96, 128), bf16),
            vmem((7, 96, 128), bf16),
            vmem((4, 24, 128), bf16),
            vmem((3, 24, 128), bf16),
            vmem((D, 128), bf16),
            pltpu.SemaphoreType.DMA((10,)),
            pltpu.SemaphoreType.DMA((20,)),
            pltpu.SemaphoreType.DMA((9,)),
            pltpu.SemaphoreType.DMA((4,)),
        ],
        compiler_params=pltpu.CompilerParams(
            collective_id=0, has_side_effects=True, vmem_limit_bytes=48 * 1024 * 1024
        ),
        name="layer",
    )(
        *(
            pltpu.with_memory_space_constraint(value, pltpu.HBM)
            for value in (
                tokens.reshape(512, D), cotangent.reshape(512, D), clear_flags.reshape(32, 16),
                time_project, time_output, column_project, column_output, date_numbers, decay_slopes,
            )
        )
    )
    mixed, project_grad, output_grad = pl.pallas_call(
        finish_kernel,
        out_shape=(
            jax.ShapeDtypeStruct((512, D), bf16),
            jax.ShapeDtypeStruct((18, 48), f32),
            jax.ShapeDtypeStruct((6, 48), f32),
        ),
        in_specs=[VM] * 2,
        out_specs=(VM, VM, VM),
        compiler_params=pltpu.CompilerParams(vmem_limit_bytes=8 * 1024 * 1024),
        name="finish",
    )(recv_c, r4)
    return mixed.reshape(tokens.shape), project_grad.T, output_grad.T


def solution(mesh):
    return jax.shard_map(
        body,
        mesh=mesh,
        in_specs=(
            P("date", "row", None, None), P("date", "row", None), P("date"),
            P(), P(), P(), P(), P(), P("date", "row", None, None),
        ),
        out_specs=(P("date", "row", None, None), P("row", "date"), P("row", "date")),
        check_vma=False,
    )
```

```python
import functools
import math

import jax
import jax.numpy as jnp
from jax import lax
from jax.experimental import pallas as pl
from jax.experimental.pallas import tpu as pltpu
from jax.sharding import PartitionSpec as P

MESH = pl.DeviceIdType.MESH
epsilon = 1e-06
masked_score = -1e30
D = 384
HEADS = 12
GROUPS = 3
inverse_root = 1.0 / math.sqrt(D // HEADS)
bf16, f32 = jnp.bfloat16, jnp.float32


def iota(shape, axis):
    return lax.broadcasted_iota(jnp.int32, shape, axis)


def one_hot(source, width):
    lanes = iota((source.shape[0], width), 1)
    return jnp.where(lanes == source, 1.0, 0.0).astype(bf16)


def matmul(left, right):
    return jnp.dot(left, right, preferred_element_type=f32)


def contract_rows(left, right):
    return lax.dot_general(left, right, (((0,), (0,)), ((), ())), preferred_element_type=f32)


def contract_last(left, right):
    return lax.dot_general(left, right, (((1,), (1,)), ((), ())), preferred_element_type=f32)


def rms_norm(values):
    widened = values.astype(f32)
    factor = lax.rsqrt(jnp.mean(widened * widened, axis=-1, keepdims=True) + epsilon)
    return (widened * factor).astype(bf16)


def head_masks():
    lanes = iota((128, 128), 1) >> 5
    return [lanes == head for head in range(4)]


def stacked(block, masks):
    return jnp.concatenate([jnp.where(mask, block, jnp.zeros_like(block)) for mask in masks], axis=0)


def unstacked(blocks, masks):
    total = jnp.where(masks[0], blocks[0:128], 0.0)
    for head in range(1, 4):
        total = jnp.where(masks[head], blocks[128 * head : 128 * head + 128], total)
    return total


def softmax_block(scores):
    raised = jnp.exp(scores - jnp.max(scores, axis=-1, keepdims=True))
    return raised * (1.0 / jnp.sum(raised, axis=-1, keepdims=True))


def signal(device):
    pl.semaphore_signal(
        pltpu.get_barrier_semaphore(), inc=1, device_id=device, device_id_type=MESH
    )


def remote(source, target, send_sem, recv_sem, device):
    return pltpu.make_async_remote_copy(
        src_ref=source,
        dst_ref=target,
        send_sem=send_sem,
        recv_sem=recv_sem,
        device_id=device,
        device_id_type=MESH,
    )


def wait_bytes(ref, sem):
    pltpu.make_async_copy(ref, ref, sem).wait()


def swing(step, count):
    half = lax.div(step + 1, 2)
    return jnp.where(lax.rem(step, 2) == 1, half, count - half)


def layer_kernel(
    tokens_hbm, cotangent_hbm, flags_hbm, time_project_hbm, time_output_hbm,
    column_project_hbm, column_output_hbm, numbers_hbm, slopes_hbm,
    recv_c, r4,
    tokens_ref, rc_in, flags_ref, project_ref, output_ref, column_project_ref, column_output_ref,
    numbers_ref, slopes_ref,
    sa, ra, ss, rs, sc, sb, rb_ref, rc_ref, side, gap_ref, info_ref, base, qkv, heads,
    plane, normed, heads_grad, qkv_grad, send_c, natural, partial_x, partial_y,
    s1, r1, s2x, r2x, s3x, r3x, s2y, r2y, s3y, r3y, s4,
    sem, grad_sem, load_sem, b_sem,
):
    d, r = lax.axis_index("date"), lax.axis_index("row")
    parity, octet, kk = d % 2, d // 8, (d // 2) % 4
    x, z_lo, core = d % 4, (d // 4) % 2, r % 2
    own = parity * 8 + r
    partner = (d, r + 1 - 2 * core)

    loads = [
        pltpu.make_async_copy(source, target, load_sem.at[index])
        for index, (source, target) in enumerate((
            (tokens_hbm, tokens_ref), (flags_hbm, flags_ref), (numbers_hbm, numbers_ref),
            (cotangent_hbm, rc_in), (time_project_hbm, project_ref), (slopes_hbm, slopes_ref),
            (time_output_hbm, output_ref), (column_output_hbm, column_output_ref),
            (column_project_hbm, column_project_ref),
        ))
    ]
    for load in loads:
        load.start()

    def greet_same_row(step, carry):
        signal((lax.rem(d + step, 64), r))
        return carry

    def greet_targets(step, carry):
        signal((2 * step + parity, octet))
        signal((8 * r + 2 * lax.div(step, 8) + parity, lax.rem(step, 8)))
        return carry

    def greet_columns(step, carry):
        to = lax.rem(own + step, 16)
        signal((d - parity + lax.div(to, 8), lax.rem(to, 8)))
        return carry

    lax.fori_loop(1, 64, greet_same_row, 0, unroll=9)
    lax.fori_loop(0, 32, greet_targets, 0, unroll=8)
    lax.fori_loop(1, 16, greet_columns, 0, unroll=5)
    signal(partner)
    for index in range(8):
        signal((d - 4 * z_lo + 4 * core, index))
        signal((d - 4 * z_lo + 4 * (index % 2), index - index % 2 + z_lo))

    row = iota((512, 1), 0)
    loads[0].wait()
    target = row >> 3
    column = (target & 1) * 8 + (target >> 3)
    source = ((row >> 2) & 1) * 256 + (((target >> 1) & 3) * 4 + (row & 3)) * 16 + column
    sa[...] = matmul(one_hot(source, 512), tokens_ref[...]).astype(bf16).reshape(64, 8, D)
    loads[1].wait()
    flipped = contract_rows(
        flags_ref[...].astype(f32).astype(bf16), one_hot(iota((32, 1), 0), 128)
    )
    loads[2].wait()
    lane = iota((1, 128), 1)
    first, second = numbers_ref[0], numbers_ref[1]
    extra = jnp.where(lane == 32, first // 32, 0) + jnp.where(lane == 33, second // 32, 0)
    extra = extra + jnp.where(lane == 34, first % 32, 0) + jnp.where(lane == 35, second % 32, 0)
    flipped = flipped + extra.astype(f32)
    for index in range(16):
        ss[index] = flipped[index : index + 1]

    pl.semaphore_wait(pltpu.get_barrier_semaphore(), 63 + 64 + 15 + 1 + 16)

    def send_tokens(step, carry):
        to = lax.rem(d + swing(step, 64), 64)
        remote(sa.at[to], ra.at[d], sem.at[0], sem.at[1], (to, r)).start()
        return carry

    def send_side(step, carry):
        to = lax.rem(d + swing(step, 64), 64)
        side_of = lax.rem(to, 2) * 8 + lax.div(to, 8)
        remote(ss.at[side_of], rs.at[d], sem.at[2], sem.at[3], (to, r)).start()
        return carry

    def send_cotangent(step, carry):
        to = lax.rem(own + step, 16)
        for when in range(2):
            remote(
                sc.at[2 * to + when],
                rc_ref.at[2 * parity + when, pl.ds(pl.multiple_of(16 * r, 16), 16)],
                sem.at[4], sem.at[5], (d - parity + lax.div(to, 8), lax.rem(to, 8)),
            ).start()
        return carry

    lax.fori_loop(1, 64, send_tokens, 0, unroll=3)
    pltpu.make_async_copy(sa.at[d], ra.at[d], sem.at[1]).start()
    lax.fori_loop(1, 64, send_side, 0)
    pltpu.make_async_copy(ss.at[parity * 8 + octet], rs.at[d], sem.at[3]).start()
    loads[3].wait()
    source = ((row >> 4) & 1) * 256 + (row & 15) * 16 + (row >> 5)
    sc[...] = matmul(one_hot(source, 512), rc_in[...]).astype(bf16).reshape(32, 16, D)
    lax.fori_loop(1, 16, send_cotangent, 0)
    for when in range(2):
        pltpu.make_async_copy(
            sc.at[2 * own + when],
            rc_ref.at[2 * parity + when, pl.ds(pl.multiple_of(16 * r, 16), 16)],
            sem.at[5],
        ).start()
    for load in loads[4:]:
        load.wait()

    wait_bytes(ra, sem.at[1])
    source = ((row & 31) * 2 + ((row >> 6) & 1)) * 8 + ((row >> 5) & 1) * 4 + (row >> 7)
    ordered = matmul(one_hot(source, 512), ra[...].reshape(512, D)).astype(bf16)
    for piece in range(16):
        patch, part = piece // 4, piece % 4
        base[part, 32 * patch : 32 * patch + 32] = ordered[32 * piece : 32 * piece + 32]
    qkv[...] = matmul(rms_norm(ordered), project_ref[...]).astype(bf16)

    wait_bytes(rs, sem.at[3])
    for index in range(64):
        side[index : index + 1] = rs[index]
    side_low = side[...].astype(bf16)
    info = jnp.zeros((8, 128), f32)
    pick_row, pick_lane = iota((8, 128), 0), iota((8, 128), 1)
    for when in range(2):
        wanted = jnp.where(pick_row < 4, when * 16 + 4 * kk + pick_row, 32 + when + 2 * (pick_row - 4))
        picked = contract_last(jnp.where(pick_lane == wanted, 1.0, 0.0).astype(bf16), side_low)
        giver = iota((64, 128), 0)
        place = (giver & 1) * 64 + when * 32 + (giver >> 1)
        spread = jnp.where(iota((64, 128), 1) == place, 1.0, 0.0).astype(bf16)
        info = info + matmul(picked.astype(bf16), spread)
    info_ref[...] = info
    days = info[4:5] * 32.0 + info[5:6]
    same_date = iota((128, 128), 0) == iota((128, 128), 1)
    days_down = jnp.sum(jnp.where(same_date, days, 0.0), axis=1, keepdims=True)
    gap_ref[...] = jnp.abs(days_down - days)

    def time_patch(half, patch):
        rows = pl.ds(pl.multiple_of(patch * 128 + half * 32, 32), 32)
        keys_rows = pl.ds(pl.multiple_of(patch * 128, 128), 128)
        out_rows = pl.ds(pl.multiple_of(patch * 32, 32), 32)
        masks = head_masks()
        allowed = (info_ref[pl.ds(patch, 1), :] > 0.5) | (
            iota((32, 128), 0) + 32 * half == iota((32, 128), 1)
        )
        gap = gap_ref[pl.ds(pl.multiple_of(half * 32, 32), 32), :]
        for group in range(GROUPS):
            queries = qkv[rows, 128 * group : 128 * group + 128]
            keys = stacked(qkv[keys_rows, D + 128 * group : D + 128 * group + 128], masks)
            values = stacked(qkv[keys_rows, 2 * D + 128 * group : 2 * D + 128 * group + 128], masks)
            scores = contract_last(queries, keys)
            weights = []
            for head in range(4):
                block = scores[:, 128 * head : 128 * head + 128] * inverse_root
                block = block + (-slopes_ref[4 * group + head]) * gap
                block = jnp.where(allowed, block, masked_score)
                weights.append(softmax_block(block).astype(bf16))
            heads[out_rows, 128 * group : 128 * group + 128] = matmul(
                jnp.concatenate(weights, axis=1), values
            ).astype(bf16)

    slot = 4 * r + kk
    home = r == octet

    def time_half(half, carry):
        def time_pair(pair, inner):
            time_patch(half, 2 * pair)
            time_patch(half, 2 * pair + 1)
            return inner

        lax.fori_loop(0, 2, time_pair, 0)
        hidden = (
            base[half].astype(f32) + matmul(heads[0:128, :], output_ref[...])
        ).astype(bf16)
        small = iota((128, 1), 0)
        source = (small & 3) * 32 + (small >> 2)
        sb[half] = matmul(one_hot(source, 128), hidden).reshape(32, 4, D).astype(bf16)

        def send_hidden(step, inner):
            to = lax.rem(lax.div(d, 2) + swing(step, 32), 32)
            remote(
                sb.at[half, to], rb_ref.at[half, slot], b_sem.at[half], b_sem.at[4 + half],
                (2 * to + parity, octet),
            ).start()
            return inner

        lax.fori_loop(1, 32, send_hidden, 0)

        @pl.when(home)
        def _():
            pltpu.make_async_copy(sb.at[half, d // 2], rb_ref.at[half, slot], b_sem.at[4 + half]).start()

        @pl.when(jnp.logical_not(home))
        def _():
            remote(
                sb.at[half, d // 2], rb_ref.at[half, slot], b_sem.at[half], b_sem.at[4 + half], (d, octet)
            ).start()

        return carry

    lax.fori_loop(0, 4, time_half, 0)

    wait_bytes(rc_ref, sem.at[5])
    heads_grad[...] = contract_last(rc_ref[...].reshape(512, D), column_output_ref[...]).astype(bf16)
    def column_date(date, carry):
        rows = pl.ds(pl.multiple_of(date * 128, 128), 128)
        masks = head_masks()
        for group in range(GROUPS):
            lanes = slice(128 * group, 128 * group + 128)
            queries = qkv[rows, 128 * group : 128 * group + 128]
            keys = stacked(qkv[rows, D + 128 * group : D + 128 * group + 128], masks)
            values = stacked(qkv[rows, 2 * D + 128 * group : 2 * D + 128 * group + 128], masks)
            outer = heads_grad[rows, lanes]
            scores = contract_last(queries, keys)
            products = contract_last(outer, values)
            weights_low, scores_low = [], []
            for head in range(4):
                weights = softmax_block(scores[:, 128 * head : 128 * head + 128] * inverse_root)
                product = products[:, 128 * head : 128 * head + 128]
                centre = jnp.sum(weights * product, axis=-1, keepdims=True)
                weights_low.append(weights.astype(bf16))
                scores_low.append((weights * (product - centre)).astype(bf16))
            low = jnp.concatenate(weights_low, axis=1)
            score_low = jnp.concatenate(scores_low, axis=1)
            heads[rows, lanes] = matmul(low, values).astype(bf16)
            qkv_grad[rows, 128 * group : 128 * group + 128] = (
                matmul(score_low, keys) * inverse_root
            ).astype(bf16)
            qkv_grad[rows, D + 128 * group : D + 128 * group + 128] = (
                unstacked(contract_rows(score_low, queries), masks) * inverse_root
            ).astype(bf16)
            qkv_grad[rows, 2 * D + 128 * group : 2 * D + 128 * group + 128] = unstacked(
                contract_rows(low, outer), masks
            ).astype(bf16)
        return carry

    def send_mixed(date, carry):
        rows = pl.ds(pl.multiple_of(date * 128, 128), 128)
        mixed = plane[rows, :].astype(f32) + matmul(heads[rows, :], column_output_ref[...])
        send_c[date] = mixed.astype(bf16).reshape(8, 16, D)
        to_date = d - parity + date // 2

        def send_rows(step, inner):
            to = lax.rem(r + swing(step, 8), 8)
            remote(
                send_c.at[date, to], recv_c.at[date % 2, own], sem.at[8], sem.at[9], (to_date, to)
            ).start()
            return inner

        lax.fori_loop(1, 8, send_rows, 0)

        @pl.when(to_date == d)
        def _():
            pltpu.make_async_copy(send_c.at[date, r], recv_c.at[date % 2, own], sem.at[9]).start()

        @pl.when(to_date != d)
        def _():
            remote(
                send_c.at[date, r], recv_c.at[date % 2, own], sem.at[8], sem.at[9], (to_date, r)
            ).start()

        return carry

    def column_half(half, carry):
        wait_bytes(rb_ref.at[half], b_sem.at[4 + half])
        rows = pl.ds(pl.multiple_of(half * 128, 128), 128)
        hidden = rb_ref[half].reshape(128, D)
        plane[rows, :] = hidden
        column_normed = rms_norm(hidden)
        normed[rows, :] = column_normed
        qkv[rows, :] = matmul(column_normed, column_project_ref[...]).astype(bf16)
        column_date(half, 0)

        @pl.when(half < 2)
        def _():
            send_mixed(half, 0)

        return carry

    lax.fori_loop(0, 4, column_half, 0)

    natural[0:1152] = contract_rows(qkv_grad[...], normed[...])
    natural[1152:1536] = contract_rows(rc_ref[...].reshape(512, D), heads[...])
    for block in range(64):
        bits = (block % 8) * 8 + (block // 32) * 4 + (block // 8) % 4
        flipped_block = (block // 32) * 32 + (block % 8) * 4 + (block // 8) % 4
        partial_y[flipped_block, 0:18] = natural[18 * bits : 18 * bits + 18, 256:384]
        partial_y[flipped_block, 18:24] = natural[1152 + 6 * bits : 1152 + 6 * bits + 6, 256:384]
        partial_x[block, 0:18] = natural[18 * bits : 18 * bits + 18, 0:256]
        partial_x[block, 18:24] = natural[1152 + 6 * bits : 1152 + 6 * bits + 6, 0:256]

    along_x = (x, 4, 1, (1, 3, 2), lambda step: (d - x + (x + step) % 4, r))
    along_y = (octet, 8, 8, (1, 7, 2, 6, 3, 5, 4), lambda step: ((d + 8 * step) % 64, r))
    plans = (
        (2, partial_y, 0, along_y, s2y, r2y, along_x, s3y, r3y),
        (0, partial_x, 0, along_x, s2x.at[0], r2x.at[0], along_y, s3x.at[0], r3x.at[0]),
        (1, partial_x, 128, along_x, s2x.at[1], r2x.at[1], along_y, s3x.at[1], r3x.at[1]),
    )

    def exchange(axis, sent, received, send_sem, recv_sem):
        me, size, _, steps, device = axis
        for step in steps:
            remote(
                sent.at[(me + step) % size], received.at[step - 1], send_sem, recv_sem, device(step)
            ).start()

    def gathered(axis, sent, received, recv_sem):
        me, size = axis[:2]
        wait_bytes(received, recv_sem)
        total = sent[me].astype(f32)
        for index in range(size - 1):
            total = total + received[index].astype(f32)
        return total

    for chunk, partial, low, *_ in plans:
        other = partial[pl.ds(pl.multiple_of(32 - 32 * core, 32), 32), :, low : low + 128]
        s1[chunk] = other.reshape(768, 128).astype(bf16)
        remote(
            s1.at[chunk], r1.at[chunk], grad_sem.at[chunk], grad_sem.at[3 + chunk], partner
        ).start()
    for chunk, partial, low, first_axis, sent, received, *_ in plans:
        mine = partial[pl.ds(pl.multiple_of(32 * core, 32), 32), :, low : low + 128].reshape(768, 128)
        wait_bytes(r1.at[chunk], grad_sem.at[3 + chunk])
        size = first_axis[1]
        sent[...] = (mine + r1[chunk].astype(f32)).astype(bf16).reshape(size, 768 // size, 128)
        exchange(first_axis, sent, received, grad_sem.at[6 + chunk], grad_sem.at[9 + chunk])
    lax.fori_loop(2, 4, send_mixed, 0)
    for chunk, _, _, first_axis, sent, received, second_axis, sent_next, received_next in plans:
        total = gathered(first_axis, sent, received, grad_sem.at[9 + chunk])
        sent_next[...] = total.reshape(second_axis[1], 24, 128).astype(bf16)
        exchange(
            second_axis, sent_next, received_next, grad_sem.at[12 + chunk], grad_sem.at[15 + chunk]
        )
    for chunk, _, _, _, _, _, second_axis, sent_next, received_next in plans:
        total = gathered(second_axis, sent_next, received_next, grad_sem.at[15 + chunk])
        square = jnp.concatenate([total, jnp.zeros((104, 128), f32)], axis=0)
        s4[128 * chunk : 128 * chunk + 128] = jnp.transpose(square).astype(bf16)
    z_slot = (r // 2) * 2 + z_lo
    final_date = d - 4 * z_lo + 4 * core

    def send_final(step, carry):
        to = (r + swing(step, 8)) % 8
        remote(
            s4.at[pl.ds(pl.multiple_of(48 * to, 16), 48)], r4.at[z_slot],
            grad_sem.at[18], grad_sem.at[19], (final_date, to),
        ).start()
        return carry

    lax.fori_loop(1, 8, send_final, 0)
    mine_last = s4.at[pl.ds(pl.multiple_of(48 * r, 16), 48)]

    @pl.when(final_date == d)
    def _():
        pltpu.make_async_copy(mine_last, r4.at[z_slot], grad_sem.at[19]).start()

    @pl.when(final_date != d)
    def _():
        remote(
            mine_last, r4.at[z_slot], grad_sem.at[18], grad_sem.at[19], (final_date, r)
        ).start()

    wait_bytes(sa.at[pl.ds(0, 63)], sem.at[0])
    wait_bytes(rs.at[pl.ds(0, 63)], sem.at[2])
    wait_bytes(sc.at[pl.ds(0, 30)], sem.at[4])
    for half in range(4):
        wait_bytes(sb.at[half, pl.ds(0, 31)], b_sem.at[half])

    @pl.when(jnp.logical_not(home))
    def _():
        for half in range(4):
            wait_bytes(sb.at[half, 0], b_sem.at[half])

    wait_bytes(send_c.at[pl.ds(0, 3)], sem.at[8])
    wait_bytes(send_c.at[3, pl.ds(0, 6)], sem.at[8])
    for chunk, _, _, first_axis, sent, received, second_axis, sent_next, received_next in plans:
        wait_bytes(s1.at[chunk], grad_sem.at[chunk])
        wait_bytes(received, grad_sem.at[6 + chunk])
        wait_bytes(received_next, grad_sem.at[12 + chunk])
    wait_bytes(recv_c, sem.at[9])
    wait_bytes(r4, grad_sem.at[19])
    wait_bytes(r4.at[pl.ds(0, 7)], grad_sem.at[18])

    @pl.when(final_date != d)
    def _():
        wait_bytes(r4.at[0], grad_sem.at[18])


def finish_kernel(recv_c, r4, mixed_ref, project_grad_ref, output_grad_ref):
    small = iota((256, 1), 0)
    order = one_hot((small & 15) * 16 + (small >> 4), 256)
    for when in range(2):
        mixed_ref[256 * when : 256 * when + 256] = matmul(
            order, recv_c[when].reshape(256, D)
        ).astype(bf16)
    total = r4[0].astype(f32)
    for index in range(1, 8):
        total = total + r4[index].astype(f32)
    turned = jnp.transpose(jnp.concatenate([total, jnp.zeros((80, 128), f32)], axis=0))
    project_grad_ref[...] = turned[0:18, 0:48]
    output_grad_ref[...] = turned[18:24, 0:48]


VM = pl.BlockSpec(memory_space=pltpu.VMEM)
HB = pl.BlockSpec(memory_space=pltpu.HBM)


def body(
    tokens, clear_flags, date_numbers, decay_slopes, time_project, time_output,
    column_project, column_output, cotangent,
):
    vmem = pltpu.VMEM
    recv_c, r4 = pl.pallas_call(
        layer_kernel,
        out_shape=(
            jax.ShapeDtypeStruct((2, 16, 16, D), bf16),
            jax.ShapeDtypeStruct((8, 48, 128), bf16),
        ),
        in_specs=[HB] * 9,
        out_specs=(VM, VM),
        scratch_shapes=[
            vmem((512, D), bf16),
            vmem((512, D), bf16),
            vmem((32, 16), jnp.int32),
            vmem((D, 3 * D), bf16),
            vmem((D, D), bf16),
            vmem((D, 3 * D), bf16),
            vmem((D, D), bf16),
            pltpu.SMEM((2,), jnp.int32),
            pltpu.SMEM((HEADS,), f32),
            vmem((64, 8, D), bf16),
            vmem((64, 8, D), bf16),
            vmem((16, 1, 128), f32),
            vmem((64, 1, 128), f32),
            vmem((32, 16, D), bf16),
            vmem((4, 32, 4, D), bf16),
            vmem((4, 32, 4, D), bf16),
            vmem((4, 128, D), bf16),
            vmem((64, 128), f32),
            vmem((128, 128), f32),
            vmem((8, 128), f32),
            vmem((4, 128, D), bf16),
            vmem((512, 3 * D), bf16),
            vmem((512, D), bf16),
            vmem((512, D), bf16),
            vmem((512, D), bf16),
            vmem((512, D), bf16),
            vmem((512, 3 * D), bf16),
            vmem((4, 8, 16, D), bf16),
            vmem((1536, D), f32),
            vmem((64, 24, 256), f32),
            vmem((64, 24, 128), f32),
            vmem((3, 768, 128), bf16),
            vmem((3, 768, 128), bf16),
            vmem((2, 4, 192, 128), bf16),
            vmem((2, 3, 192, 128), bf16),
            vmem((2, 8, 24, 128), bf16),
            vmem((2, 7, 24, 128), bf16),
            vmem((8, 96, 128), bf16),
            vmem((7, 96, 128), bf16),
            vmem((4, 24, 128), bf16),
            vmem((3, 24, 128), bf16),
            vmem((D, 128), bf16),
            pltpu.SemaphoreType.DMA((10,)),
            pltpu.SemaphoreType.DMA((20,)),
            pltpu.SemaphoreType.DMA((9,)),
            pltpu.SemaphoreType.DMA((8,)),
        ],
        compiler_params=pltpu.CompilerParams(
            collective_id=0, has_side_effects=True, vmem_limit_bytes=48 * 1024 * 1024
        ),
        name="layer",
    )(
        *(
            pltpu.with_memory_space_constraint(value, pltpu.HBM)
            for value in (
                tokens.reshape(512, D), cotangent.reshape(512, D), clear_flags.reshape(32, 16),
                time_project, time_output, column_project, column_output, date_numbers, decay_slopes,
            )
        )
    )
    mixed, project_grad, output_grad = pl.pallas_call(
        finish_kernel,
        out_shape=(
            jax.ShapeDtypeStruct((512, D), bf16),
            jax.ShapeDtypeStruct((18, 48), f32),
            jax.ShapeDtypeStruct((6, 48), f32),
        ),
        in_specs=[VM] * 2,
        out_specs=(VM, VM, VM),
        compiler_params=pltpu.CompilerParams(vmem_limit_bytes=8 * 1024 * 1024),
        name="finish",
    )(recv_c, r4)
    return mixed.reshape(tokens.shape), project_grad.T, output_grad.T


def solution(mesh):
    return jax.shard_map(
        body,
        mesh=mesh,
        in_specs=(
            P("date", "row", None, None), P("date", "row", None), P("date"),
            P(), P(), P(), P(), P(), P("date", "row", None, None),
        ),
        out_specs=(P("date", "row", None, None), P("row", "date"), P("row", "date")),
        check_vma=False,
    )
```

```python
import functools
import math

import jax
import jax.numpy as jnp
from jax import lax
from jax.experimental import pallas as pl
from jax.experimental.pallas import tpu as pltpu
from jax.sharding import PartitionSpec as P

MESH = pl.DeviceIdType.MESH
epsilon = 1e-06
masked_score = -1e30
D = 384
HEADS = 12
GROUPS = 3
inverse_root = 1.0 / math.sqrt(D // HEADS)
bf16, f32 = jnp.bfloat16, jnp.float32


def iota(shape, axis):
    return lax.broadcasted_iota(jnp.int32, shape, axis)


def one_hot(source, width):
    lanes = iota((source.shape[0], width), 1)
    return jnp.where(lanes == source, 1.0, 0.0).astype(bf16)


def matmul(left, right):
    return jnp.dot(left, right, preferred_element_type=f32)


def contract_rows(left, right):
    return lax.dot_general(left, right, (((0,), (0,)), ((), ())), preferred_element_type=f32)


def contract_last(left, right):
    return lax.dot_general(left, right, (((1,), (1,)), ((), ())), preferred_element_type=f32)


def rms_norm(values):
    widened = values.astype(f32)
    factor = lax.rsqrt(jnp.mean(widened * widened, axis=-1, keepdims=True) + epsilon)
    return (widened * factor).astype(bf16)


def head_masks():
    lanes = iota((128, 128), 1) >> 5
    return [lanes == head for head in range(4)]


def stacked(block, masks):
    return jnp.concatenate([jnp.where(mask, block, jnp.zeros_like(block)) for mask in masks], axis=0)


def unstacked(blocks, masks):
    total = jnp.where(masks[0], blocks[0:128], 0.0)
    for head in range(1, 4):
        total = jnp.where(masks[head], blocks[128 * head : 128 * head + 128], total)
    return total


def softmax_block(scores, scale=1.0):
    raised = jnp.exp2((scores - jnp.max(scores, axis=-1, keepdims=True)) * (scale * math.log2(math.e)))
    return raised * (1.0 / jnp.sum(raised, axis=-1, keepdims=True))


def signal(device):
    pl.semaphore_signal(
        pltpu.get_barrier_semaphore(), inc=1, device_id=device, device_id_type=MESH
    )


def remote(source, target, send_sem, recv_sem, device):
    return pltpu.make_async_remote_copy(
        src_ref=source,
        dst_ref=target,
        send_sem=send_sem,
        recv_sem=recv_sem,
        device_id=device,
        device_id_type=MESH,
    )


def wait_bytes(ref, sem):
    pltpu.make_async_copy(ref, ref, sem).wait()


def swing(step, count):
    half = lax.div(step + 1, 2)
    return jnp.where(lax.rem(step, 2) == 1, half, count - half)


def layer_kernel(
    tokens_hbm, cotangent_hbm, flags_hbm, time_project_hbm, time_output_hbm,
    column_project_hbm, column_output_hbm, numbers_hbm, slopes_hbm,
    recv_c, r4,
    tokens_ref, rc_in, flags_ref, project_ref, output_ref, column_project_ref, column_output_ref,
    numbers_ref, slopes_ref,
    sa, ra, ss, rs, sc, sb, rb_ref, rc_ref, side, gap_ref, info_ref, base, qkv, heads,
    plane, normed, heads_grad, qkv_grad, send_c, natural, partial_x, partial_y,
    s1, r1, s2x, r2x, s3x, r3x, s2y, r2y, s3y, r3y, s4,
    sem, grad_sem, load_sem, b_sem,
):
    d, r = lax.axis_index("date"), lax.axis_index("row")
    parity, octet, kk = d % 2, d // 8, (d // 2) % 4
    x, z_lo, core = d % 4, (d // 4) % 2, r % 2
    own = parity * 8 + r
    partner = (d, r + 1 - 2 * core)

    loads = [
        pltpu.make_async_copy(source, target, load_sem.at[index])
        for index, (source, target) in enumerate((
            (tokens_hbm, tokens_ref), (flags_hbm, flags_ref), (numbers_hbm, numbers_ref),
            (cotangent_hbm, rc_in), (time_project_hbm, project_ref), (slopes_hbm, slopes_ref),
            (time_output_hbm, output_ref), (column_output_hbm, column_output_ref),
            (column_project_hbm, column_project_ref),
        ))
    ]
    for load in loads:
        load.start()

    def greet_same_row(step, carry):
        signal((lax.rem(d + step, 64), r))
        return carry

    def greet_targets(step, carry):
        signal((2 * step + parity, octet))
        signal((8 * r + 2 * lax.div(step, 8) + parity, lax.rem(step, 8)))
        return carry

    def greet_columns(step, carry):
        to = lax.rem(own + step, 16)
        signal((d - parity + lax.div(to, 8), lax.rem(to, 8)))
        return carry

    lax.fori_loop(1, 64, greet_same_row, 0, unroll=9)
    lax.fori_loop(0, 32, greet_targets, 0, unroll=8)
    lax.fori_loop(1, 16, greet_columns, 0, unroll=5)
    signal(partner)
    for index in range(8):
        signal((d - 4 * z_lo + 4 * core, index))
        signal((d - 4 * z_lo + 4 * (index % 2), index - index % 2 + z_lo))

    row = iota((512, 1), 0)
    loads[0].wait()
    target = row >> 3
    column = (target & 1) * 8 + (target >> 3)
    source = ((row >> 2) & 1) * 256 + (((target >> 1) & 3) * 4 + (row & 3)) * 16 + column
    sa[...] = matmul(one_hot(source, 512), tokens_ref[...]).astype(bf16).reshape(64, 8, D)
    loads[1].wait()
    flipped = contract_rows(
        flags_ref[...].astype(f32).astype(bf16), one_hot(iota((32, 1), 0), 128)
    )
    loads[2].wait()
    lane = iota((1, 128), 1)
    first, second = numbers_ref[0], numbers_ref[1]
    extra = jnp.where(lane == 32, first // 32, 0) + jnp.where(lane == 33, second // 32, 0)
    extra = extra + jnp.where(lane == 34, first % 32, 0) + jnp.where(lane == 35, second % 32, 0)
    flipped = flipped + extra.astype(f32)
    for index in range(16):
        ss[index] = flipped[index : index + 1]

    pl.semaphore_wait(pltpu.get_barrier_semaphore(), 63 + 64 + 15 + 1 + 16)

    def send_tokens(step, carry):
        to = lax.rem(d + swing(step, 64), 64)
        remote(sa.at[to], ra.at[d], sem.at[0], sem.at[1], (to, r)).start()
        return carry

    def send_side(step, carry):
        to = lax.rem(d + swing(step, 64), 64)
        side_of = lax.rem(to, 2) * 8 + lax.div(to, 8)
        remote(ss.at[side_of], rs.at[d], sem.at[2], sem.at[3], (to, r)).start()
        return carry

    def send_cotangent(step, carry):
        to = lax.rem(own + step, 16)
        for when in range(2):
            remote(
                sc.at[2 * to + when],
                rc_ref.at[2 * parity + when, pl.ds(pl.multiple_of(16 * r, 16), 16)],
                sem.at[4], sem.at[5], (d - parity + lax.div(to, 8), lax.rem(to, 8)),
            ).start()
        return carry

    lax.fori_loop(1, 64, send_tokens, 0, unroll=3)
    pltpu.make_async_copy(sa.at[d], ra.at[d], sem.at[1]).start()
    lax.fori_loop(1, 64, send_side, 0)
    pltpu.make_async_copy(ss.at[parity * 8 + octet], rs.at[d], sem.at[3]).start()
    loads[3].wait()
    source = ((row >> 4) & 1) * 256 + (row & 15) * 16 + (row >> 5)
    sc[...] = matmul(one_hot(source, 512), rc_in[...]).astype(bf16).reshape(32, 16, D)
    lax.fori_loop(1, 16, send_cotangent, 0)
    for when in range(2):
        pltpu.make_async_copy(
            sc.at[2 * own + when],
            rc_ref.at[2 * parity + when, pl.ds(pl.multiple_of(16 * r, 16), 16)],
            sem.at[5],
        ).start()
    for load in loads[4:]:
        load.wait()

    wait_bytes(ra, sem.at[1])
    source = (((row >> 1) & 31) * 2 + ((row >> 6) & 1)) * 8 + (row & 1) * 4 + (row >> 7)
    ordered = matmul(one_hot(source, 512), ra[...].reshape(512, D)).astype(bf16)
    for piece in range(8):
        patch, half = piece // 2, piece % 2
        base[half, 64 * patch : 64 * patch + 64] = ordered[64 * piece : 64 * piece + 64]
    qkv[...] = matmul(rms_norm(ordered), project_ref[...]).astype(bf16)

    wait_bytes(rs, sem.at[3])
    for index in range(64):
        side[index : index + 1] = rs[index]
    side_low = side[...].astype(bf16)
    info = jnp.zeros((8, 128), f32)
    pick_row, pick_lane = iota((8, 128), 0), iota((8, 128), 1)
    for when in range(2):
        wanted = jnp.where(pick_row < 4, when * 16 + 4 * kk + pick_row, 32 + when + 2 * (pick_row - 4))
        picked = contract_last(jnp.where(pick_lane == wanted, 1.0, 0.0).astype(bf16), side_low)
        giver = iota((64, 128), 0)
        place = (giver & 1) * 64 + (giver >> 1) * 2 + when
        spread = jnp.where(iota((64, 128), 1) == place, 1.0, 0.0).astype(bf16)
        info = info + matmul(picked.astype(bf16), spread)
    info_ref[...] = info
    days = info[4:5] * 32.0 + info[5:6]
    same_date = iota((128, 128), 0) == iota((128, 128), 1)
    days_down = jnp.sum(jnp.where(same_date, days, 0.0), axis=1, keepdims=True)
    gap_ref[...] = jnp.abs(days_down - days)

    def time_patch(half, patch):
        rows = pl.ds(pl.multiple_of(patch * 128 + half * 64, 64), 64)
        keys_rows = pl.ds(pl.multiple_of(patch * 128, 128), 128)
        out_rows = pl.ds(pl.multiple_of(patch * 64, 64), 64)
        masks = head_masks()
        allowed = (info_ref[pl.ds(patch, 1), :] > 0.5) | (
            iota((64, 128), 0) + 64 * half == iota((64, 128), 1)
        )
        gap = gap_ref[pl.ds(pl.multiple_of(half * 64, 64), 64), :]
        for group in range(GROUPS):
            queries = qkv[rows, 128 * group : 128 * group + 128]
            keys = stacked(qkv[keys_rows, D + 128 * group : D + 128 * group + 128], masks)
            values = stacked(qkv[keys_rows, 2 * D + 128 * group : 2 * D + 128 * group + 128], masks)
            scores = contract_last(queries, keys)
            weights = []
            for head in range(4):
                block = scores[:, 128 * head : 128 * head + 128] * inverse_root
                block = block + (-slopes_ref[4 * group + head]) * gap
                block = jnp.where(allowed, block, masked_score)
                weights.append(softmax_block(block).astype(bf16))
            heads[out_rows, 128 * group : 128 * group + 128] = matmul(
                jnp.concatenate(weights, axis=1), values
            ).astype(bf16)

    slot = 4 * r + kk
    home = r == octet

    def time_half(half, carry):
        def time_pair(pair, inner):
            time_patch(half, 2 * pair)
            time_patch(half, 2 * pair + 1)
            return inner

        lax.fori_loop(0, 2, time_pair, 0)
        hidden = (
            base[half].astype(f32) + matmul(heads[0:256, :], output_ref[...])
        ).astype(bf16)
        small = iota((256, 1), 0)
        source = ((small >> 1) & 3) * 64 + (small >> 3) * 2 + (small & 1)
        sb[half] = matmul(one_hot(source, 256), hidden).astype(bf16).reshape(32, 8, D)

        def send_hidden(step, inner):
            to = lax.rem(lax.div(d, 2) + swing(step, 32), 32)
            remote(
                sb.at[half, to], rb_ref.at[half, slot], b_sem.at[half], b_sem.at[2 + half],
                (2 * to + parity, octet),
            ).start()
            return inner

        lax.fori_loop(1, 32, send_hidden, 0)

        @pl.when(home)
        def _():
            pltpu.make_async_copy(sb.at[half, d // 2], rb_ref.at[half, slot], b_sem.at[2 + half]).start()

        @pl.when(jnp.logical_not(home))
        def _():
            remote(
                sb.at[half, d // 2], rb_ref.at[half, slot], b_sem.at[half], b_sem.at[2 + half], (d, octet)
            ).start()

        return carry

    lax.fori_loop(0, 2, time_half, 0)

    wait_bytes(rc_ref, sem.at[5])
    heads_grad[...] = contract_last(rc_ref[...].reshape(512, D), column_output_ref[...]).astype(bf16)
    def column_date(date, carry):
        rows = pl.ds(pl.multiple_of(date * 128, 128), 128)
        masks = head_masks()
        for group in range(GROUPS):
            lanes = slice(128 * group, 128 * group + 128)
            queries = qkv[rows, 128 * group : 128 * group + 128]
            keys = stacked(qkv[rows, D + 128 * group : D + 128 * group + 128], masks)
            values = stacked(qkv[rows, 2 * D + 128 * group : 2 * D + 128 * group + 128], masks)
            outer = heads_grad[rows, lanes]
            scores = contract_last(queries, keys)
            products = contract_last(outer, values)
            weights_low, scores_low = [], []
            for head in range(4):
                weights = softmax_block(scores[:, 128 * head : 128 * head + 128], inverse_root)
                product = products[:, 128 * head : 128 * head + 128]
                centre = jnp.sum(weights * product, axis=-1, keepdims=True)
                weights_low.append(weights.astype(bf16))
                scores_low.append((weights * (product - centre)).astype(bf16))
            low = jnp.concatenate(weights_low, axis=1)
            score_low = jnp.concatenate(scores_low, axis=1)
            heads[rows, lanes] = matmul(low, values).astype(bf16)
            qkv_grad[rows, 128 * group : 128 * group + 128] = (
                matmul(score_low, keys) * inverse_root
            ).astype(bf16)
            qkv_grad[rows, D + 128 * group : D + 128 * group + 128] = (
                unstacked(contract_rows(score_low, queries), masks) * inverse_root
            ).astype(bf16)
            qkv_grad[rows, 2 * D + 128 * group : 2 * D + 128 * group + 128] = unstacked(
                contract_rows(low, outer), masks
            ).astype(bf16)
        return carry

    def send_mixed(date, carry):
        rows = pl.ds(pl.multiple_of(date * 128, 128), 128)
        mixed = plane[rows, :].astype(f32) + matmul(heads[rows, :], column_output_ref[...])
        send_c[date] = mixed.astype(bf16).reshape(8, 16, D)
        to_date = d - parity + date // 2

        def send_rows(step, inner):
            to = lax.rem(r + swing(step, 8), 8)
            remote(
                send_c.at[date, to], recv_c.at[date % 2, own], sem.at[8], sem.at[9], (to_date, to)
            ).start()
            return inner

        lax.fori_loop(1, 8, send_rows, 0)

        @pl.when(to_date == d)
        def _():
            pltpu.make_async_copy(send_c.at[date, r], recv_c.at[date % 2, own], sem.at[9]).start()

        @pl.when(to_date != d)
        def _():
            remote(
                send_c.at[date, r], recv_c.at[date % 2, own], sem.at[8], sem.at[9], (to_date, r)
            ).start()

        return carry

    def column_half(half, carry):
        wait_bytes(rb_ref.at[half], b_sem.at[2 + half])
        rows = pl.ds(pl.multiple_of(half * 256, 256), 256)
        small = iota((256, 1), 0)
        source = (small & 127) * 2 + (small >> 7)
        hidden = matmul(one_hot(source, 256), rb_ref[half].reshape(256, D)).astype(bf16)
        plane[rows, :] = hidden
        column_normed = rms_norm(hidden)
        normed[rows, :] = column_normed
        qkv[rows, :] = matmul(column_normed, column_project_ref[...]).astype(bf16)
        lax.fori_loop(2 * half, 2 * half + 2, column_date, 0)

        @pl.when(half == 0)
        def _():
            lax.fori_loop(0, 2, send_mixed, 0)

        return carry

    lax.fori_loop(0, 2, column_half, 0)

    natural[0:1152] = contract_rows(qkv_grad[...], normed[...])
    natural[1152:1536] = contract_rows(rc_ref[...].reshape(512, D), heads[...])
    for block in range(64):
        bits = (block % 8) * 8 + (block // 32) * 4 + (block // 8) % 4
        flipped_block = (block // 32) * 32 + (block % 8) * 4 + (block // 8) % 4
        partial_y[flipped_block, 0:18] = natural[18 * bits : 18 * bits + 18, 256:384]
        partial_y[flipped_block, 18:24] = natural[1152 + 6 * bits : 1152 + 6 * bits + 6, 256:384]
        partial_x[block, 0:18] = natural[18 * bits : 18 * bits + 18, 0:256]
        partial_x[block, 18:24] = natural[1152 + 6 * bits : 1152 + 6 * bits + 6, 0:256]

    along_x = (x, 4, 1, (1, 3, 2), lambda step: (d - x + (x + step) % 4, r))
    along_y = (octet, 8, 8, (1, 7, 2, 6, 3, 5, 4), lambda step: ((d + 8 * step) % 64, r))
    plans = (
        (2, partial_y, 0, along_y, s2y, r2y, along_x, s3y, r3y),
        (0, partial_x, 0, along_x, s2x.at[0], r2x.at[0], along_y, s3x.at[0], r3x.at[0]),
        (1, partial_x, 128, along_x, s2x.at[1], r2x.at[1], along_y, s3x.at[1], r3x.at[1]),
    )

    def exchange(axis, sent, received, send_sem, recv_sem):
        me, size, _, steps, device = axis
        for step in steps:
            remote(
                sent.at[(me + step) % size], received.at[step - 1], send_sem, recv_sem, device(step)
            ).start()

    def gathered(axis, sent, received, recv_sem):
        me, size = axis[:2]
        wait_bytes(received, recv_sem)
        total = sent[me].astype(f32)
        for index in range(size - 1):
            total = total + received[index].astype(f32)
        return total

    for chunk, partial, low, *_ in plans:
        other = partial[pl.ds(pl.multiple_of(32 - 32 * core, 32), 32), :, low : low + 128]
        s1[chunk] = other.reshape(768, 128).astype(bf16)
        remote(
            s1.at[chunk], r1.at[chunk], grad_sem.at[chunk], grad_sem.at[3 + chunk], partner
        ).start()
    for chunk, partial, low, first_axis, sent, received, *_ in plans:
        mine = partial[pl.ds(pl.multiple_of(32 * core, 32), 32), :, low : low + 128].reshape(768, 128)
        wait_bytes(r1.at[chunk], grad_sem.at[3 + chunk])
        size = first_axis[1]
        sent[...] = (mine + r1[chunk].astype(f32)).astype(bf16).reshape(size, 768 // size, 128)
        exchange(first_axis, sent, received, grad_sem.at[6 + chunk], grad_sem.at[9 + chunk])
    lax.fori_loop(2, 4, send_mixed, 0)
    for chunk, _, _, first_axis, sent, received, second_axis, sent_next, received_next in plans:
        total = gathered(first_axis, sent, received, grad_sem.at[9 + chunk])
        sent_next[...] = total.reshape(second_axis[1], 24, 128).astype(bf16)
        exchange(
            second_axis, sent_next, received_next, grad_sem.at[12 + chunk], grad_sem.at[15 + chunk]
        )
    for chunk, _, _, _, _, _, second_axis, sent_next, received_next in plans:
        total = gathered(second_axis, sent_next, received_next, grad_sem.at[15 + chunk])
        square = jnp.concatenate([total, jnp.zeros((104, 128), f32)], axis=0)
        s4[128 * chunk : 128 * chunk + 128] = jnp.transpose(square).astype(bf16)
    z_slot = (r // 2) * 2 + z_lo
    final_date = d - 4 * z_lo + 4 * core

    def send_final(step, carry):
        to = (r + swing(step, 8)) % 8
        remote(
            s4.at[pl.ds(pl.multiple_of(48 * to, 16), 48)], r4.at[z_slot],
            grad_sem.at[18], grad_sem.at[19], (final_date, to),
        ).start()
        return carry

    lax.fori_loop(1, 8, send_final, 0)
    mine_last = s4.at[pl.ds(pl.multiple_of(48 * r, 16), 48)]

    @pl.when(final_date == d)
    def _():
        pltpu.make_async_copy(mine_last, r4.at[z_slot], grad_sem.at[19]).start()

    @pl.when(final_date != d)
    def _():
        remote(
            mine_last, r4.at[z_slot], grad_sem.at[18], grad_sem.at[19], (final_date, r)
        ).start()

    wait_bytes(sa.at[pl.ds(0, 63)], sem.at[0])
    wait_bytes(rs.at[pl.ds(0, 63)], sem.at[2])
    wait_bytes(sc.at[pl.ds(0, 30)], sem.at[4])
    for half in range(2):
        wait_bytes(sb.at[half, pl.ds(0, 31)], b_sem.at[half])

    @pl.when(jnp.logical_not(home))
    def _():
        for half in range(2):
            wait_bytes(sb.at[half, 0], b_sem.at[half])

    wait_bytes(send_c.at[pl.ds(0, 3)], sem.at[8])
    wait_bytes(send_c.at[3, pl.ds(0, 6)], sem.at[8])
    for chunk, _, _, first_axis, sent, received, second_axis, sent_next, received_next in plans:
        wait_bytes(s1.at[chunk], grad_sem.at[chunk])
        wait_bytes(received, grad_sem.at[6 + chunk])
        wait_bytes(received_next, grad_sem.at[12 + chunk])
    wait_bytes(recv_c, sem.at[9])
    wait_bytes(r4, grad_sem.at[19])
    wait_bytes(r4.at[pl.ds(0, 7)], grad_sem.at[18])

    @pl.when(final_date != d)
    def _():
        wait_bytes(r4.at[0], grad_sem.at[18])


def finish_kernel(recv_c, r4, mixed_ref, project_grad_ref, output_grad_ref):
    small = iota((256, 1), 0)
    order = one_hot((small & 15) * 16 + (small >> 4), 256)
    for when in range(2):
        mixed_ref[256 * when : 256 * when + 256] = matmul(
            order, recv_c[when].reshape(256, D)
        ).astype(bf16)
    total = r4[0].astype(f32)
    for index in range(1, 8):
        total = total + r4[index].astype(f32)
    turned = jnp.transpose(jnp.concatenate([total, jnp.zeros((80, 128), f32)], axis=0))
    project_grad_ref[...] = turned[0:18, 0:48]
    output_grad_ref[...] = turned[18:24, 0:48]


VM = pl.BlockSpec(memory_space=pltpu.VMEM)
HB = pl.BlockSpec(memory_space=pltpu.HBM)


def body(
    tokens, clear_flags, date_numbers, decay_slopes, time_project, time_output,
    column_project, column_output, cotangent,
):
    vmem = pltpu.VMEM
    recv_c, r4 = pl.pallas_call(
        layer_kernel,
        out_shape=(
            jax.ShapeDtypeStruct((2, 16, 16, D), bf16),
            jax.ShapeDtypeStruct((8, 48, 128), bf16),
        ),
        in_specs=[HB] * 9,
        out_specs=(VM, VM),
        scratch_shapes=[
            vmem((512, D), bf16),
            vmem((512, D), bf16),
            vmem((32, 16), jnp.int32),
            vmem((D, 3 * D), bf16),
            vmem((D, D), bf16),
            vmem((D, 3 * D), bf16),
            vmem((D, D), bf16),
            pltpu.SMEM((2,), jnp.int32),
            pltpu.SMEM((HEADS,), f32),
            vmem((64, 8, D), bf16),
            vmem((64, 8, D), bf16),
            vmem((16, 1, 128), f32),
            vmem((64, 1, 128), f32),
            vmem((32, 16, D), bf16),
            vmem((2, 32, 8, D), bf16),
            vmem((2, 32, 8, D), bf16),
            vmem((4, 128, D), bf16),
            vmem((64, 128), f32),
            vmem((128, 128), f32),
            vmem((8, 128), f32),
            vmem((2, 256, D), bf16),
            vmem((512, 3 * D), bf16),
            vmem((512, D), bf16),
            vmem((512, D), bf16),
            vmem((512, D), bf16),
            vmem((512, D), bf16),
            vmem((512, 3 * D), bf16),
            vmem((4, 8, 16, D), bf16),
            vmem((1536, D), f32),
            vmem((64, 24, 256), f32),
            vmem((64, 24, 128), f32),
            vmem((3, 768, 128), bf16),
            vmem((3, 768, 128), bf16),
            vmem((2, 4, 192, 128), bf16),
            vmem((2, 3, 192, 128), bf16),
            vmem((2, 8, 24, 128), bf16),
            vmem((2, 7, 24, 128), bf16),
            vmem((8, 96, 128), bf16),
            vmem((7, 96, 128), bf16),
            vmem((4, 24, 128), bf16),
            vmem((3, 24, 128), bf16),
            vmem((D, 128), bf16),
            pltpu.SemaphoreType.DMA((10,)),
            pltpu.SemaphoreType.DMA((20,)),
            pltpu.SemaphoreType.DMA((9,)),
            pltpu.SemaphoreType.DMA((4,)),
        ],
        compiler_params=pltpu.CompilerParams(
            collective_id=0, has_side_effects=True, vmem_limit_bytes=48 * 1024 * 1024
        ),
        name="layer",
    )(
        *(
            pltpu.with_memory_space_constraint(value, pltpu.HBM)
            for value in (
                tokens.reshape(512, D), cotangent.reshape(512, D), clear_flags.reshape(32, 16),
                time_project, time_output, column_project, column_output, date_numbers, decay_slopes,
            )
        )
    )
    mixed, project_grad, output_grad = pl.pallas_call(
        finish_kernel,
        out_shape=(
            jax.ShapeDtypeStruct((512, D), bf16),
            jax.ShapeDtypeStruct((18, 48), f32),
            jax.ShapeDtypeStruct((6, 48), f32),
        ),
        in_specs=[VM] * 2,
        out_specs=(VM, VM, VM),
        compiler_params=pltpu.CompilerParams(vmem_limit_bytes=8 * 1024 * 1024),
        name="finish",
    )(recv_c, r4)
    return mixed.reshape(tokens.shape), project_grad.T, output_grad.T


def solution(mesh):
    return jax.shard_map(
        body,
        mesh=mesh,
        in_specs=(
            P("date", "row", None, None), P("date", "row", None), P("date"),
            P(), P(), P(), P(), P(), P("date", "row", None, None),
        ),
        out_specs=(P("date", "row", None, None), P("row", "date"), P("row", "date")),
        check_vma=False,
    )
```

```python
import functools
import math

import jax
import jax.numpy as jnp
from jax import lax
from jax.experimental import pallas as pl
from jax.experimental.pallas import tpu as pltpu
from jax.sharding import PartitionSpec as P

MESH = pl.DeviceIdType.MESH
epsilon = 1e-06
masked_score = -1e30
D = 384
HEADS = 12
GROUPS = 3
inverse_root = 1.0 / math.sqrt(D // HEADS)
bf16, f32 = jnp.bfloat16, jnp.float32


def iota(shape, axis):
    return lax.broadcasted_iota(jnp.int32, shape, axis)


def one_hot(source, width):
    lanes = iota((source.shape[0], width), 1)
    return jnp.where(lanes == source, 1.0, 0.0).astype(bf16)


def matmul(left, right):
    return jnp.dot(left, right, preferred_element_type=f32)


def contract_rows(left, right):
    return lax.dot_general(left, right, (((0,), (0,)), ((), ())), preferred_element_type=f32)


def contract_last(left, right):
    return lax.dot_general(left, right, (((1,), (1,)), ((), ())), preferred_element_type=f32)


def rms_norm(values):
    widened = values.astype(f32)
    factor = lax.rsqrt(jnp.mean(widened * widened, axis=-1, keepdims=True) + epsilon)
    return (widened * factor).astype(bf16)


def head_masks():
    lanes = iota((128, 128), 1) >> 5
    return [lanes == head for head in range(4)]


def stacked(block, masks):
    return jnp.concatenate([jnp.where(mask, block, jnp.zeros_like(block)) for mask in masks], axis=0)


def unstacked(blocks, masks):
    total = jnp.where(masks[0], blocks[0:128], 0.0)
    for head in range(1, 4):
        total = jnp.where(masks[head], blocks[128 * head : 128 * head + 128], total)
    return total


def softmax_block(scores, scale=1.0):
    raised = jnp.exp2((scores - jnp.max(scores, axis=-1, keepdims=True)) * (scale * math.log2(math.e)))
    return raised * (1.0 / jnp.sum(raised, axis=-1, keepdims=True))


def signal(device):
    pl.semaphore_signal(
        pltpu.get_barrier_semaphore(), inc=1, device_id=device, device_id_type=MESH
    )


def remote(source, target, send_sem, recv_sem, device):
    return pltpu.make_async_remote_copy(
        src_ref=source,
        dst_ref=target,
        send_sem=send_sem,
        recv_sem=recv_sem,
        device_id=device,
        device_id_type=MESH,
    )


def wait_bytes(ref, sem):
    pltpu.make_async_copy(ref, ref, sem).wait()


def swing(step, count):
    half = lax.div(step + 1, 2)
    return jnp.where(lax.rem(step, 2) == 1, half, count - half)


def layer_kernel(
    tokens_hbm, cotangent_hbm, flags_hbm, time_project_hbm, time_output_hbm,
    column_project_hbm, column_output_hbm, numbers_hbm, slopes_hbm,
    recv_c, r4,
    tokens_ref, rc_in, flags_ref, project_ref, output_ref, column_project_ref, column_output_ref,
    numbers_ref, slopes_ref,
    sa, ra, ss, rs, sc, sb, rb_ref, rc_ref, side, gap_ref, info_ref, base, qkv, heads,
    plane, normed, heads_grad, qkv_grad, send_c, natural, partial_x, partial_y,
    s1, r1, s2x, r2x, s3x, r3x, s2y, r2y, s3y, r3y, s4,
    sem, grad_sem, load_sem, b_sem,
):
    d, r = lax.axis_index("date"), lax.axis_index("row")
    parity, octet, kk = d % 2, d // 8, (d // 2) % 4
    x, z_lo, core = d % 4, (d // 4) % 2, r % 2
    own = parity * 8 + r
    partner = (d, r + 1 - 2 * core)

    loads = [
        pltpu.make_async_copy(source, target, load_sem.at[index])
        for index, (source, target) in enumerate((
            (tokens_hbm, tokens_ref), (flags_hbm, flags_ref), (numbers_hbm, numbers_ref),
            (cotangent_hbm, rc_in), (time_project_hbm, project_ref), (slopes_hbm, slopes_ref),
            (time_output_hbm, output_ref), (column_output_hbm, column_output_ref),
            (column_project_hbm, column_project_ref),
        ))
    ]
    for load in loads:
        load.start()

    def greet_same_row(step, carry):
        signal((lax.rem(d + step, 64), r))
        return carry

    def greet_targets(step, carry):
        signal((2 * step + parity, octet))
        signal((8 * r + 2 * lax.div(step, 8) + parity, lax.rem(step, 8)))
        return carry

    def greet_columns(step, carry):
        to = lax.rem(own + step, 16)
        signal((d - parity + lax.div(to, 8), lax.rem(to, 8)))
        return carry

    lax.fori_loop(1, 64, greet_same_row, 0, unroll=9)
    lax.fori_loop(0, 32, greet_targets, 0, unroll=8)
    lax.fori_loop(1, 16, greet_columns, 0, unroll=5)
    signal(partner)
    for index in range(8):
        signal((d - 4 * z_lo + 4 * core, index))
        signal((d - 4 * z_lo + 4 * (index % 2), index - index % 2 + z_lo))

    row = iota((512, 1), 0)
    loads[0].wait()
    target = row >> 3
    column = (target & 1) * 8 + (target >> 3)
    source = ((row >> 2) & 1) * 256 + (((target >> 1) & 3) * 4 + (row & 3)) * 16 + column
    sa[...] = matmul(one_hot(source, 512), tokens_ref[...]).astype(bf16).reshape(64, 8, D)
    loads[1].wait()
    flipped = contract_rows(
        flags_ref[...].astype(f32).astype(bf16), one_hot(iota((32, 1), 0), 128)
    )
    loads[2].wait()
    lane = iota((1, 128), 1)
    first, second = numbers_ref[0], numbers_ref[1]
    extra = jnp.where(lane == 32, first // 32, 0) + jnp.where(lane == 33, second // 32, 0)
    extra = extra + jnp.where(lane == 34, first % 32, 0) + jnp.where(lane == 35, second % 32, 0)
    flipped = flipped + extra.astype(f32)
    for index in range(16):
        ss[index] = flipped[index : index + 1]

    pl.semaphore_wait(pltpu.get_barrier_semaphore(), 63 + 64 + 15 + 1 + 16)

    def send_tokens(step, carry):
        to = lax.rem(d + swing(step, 64), 64)
        remote(sa.at[to], ra.at[d], sem.at[0], sem.at[1], (to, r)).start()
        return carry

    def send_side(step, carry):
        to = lax.rem(d + swing(step, 64), 64)
        side_of = lax.rem(to, 2) * 8 + lax.div(to, 8)
        remote(ss.at[side_of], rs.at[d], sem.at[2], sem.at[3], (to, r)).start()
        return carry

    def send_cotangent(when):
        def send_one(step, carry):
            to = lax.rem(own + step, 16)
            remote(
                sc.at[2 * to + when],
                rc_ref.at[2 * parity + when, pl.ds(pl.multiple_of(16 * r, 16), 16)],
                sem.at[4], sem.at[5], (d - parity + lax.div(to, 8), lax.rem(to, 8)),
            ).start()
            return carry

        lax.fori_loop(1, 16, send_one, 0)
        pltpu.make_async_copy(
            sc.at[2 * own + when],
            rc_ref.at[2 * parity + when, pl.ds(pl.multiple_of(16 * r, 16), 16)],
            sem.at[5],
        ).start()

    lax.fori_loop(1, 64, send_tokens, 0, unroll=3)
    pltpu.make_async_copy(sa.at[d], ra.at[d], sem.at[1]).start()
    lax.fori_loop(1, 64, send_side, 0)
    pltpu.make_async_copy(ss.at[parity * 8 + octet], rs.at[d], sem.at[3]).start()
    loads[3].wait()
    source = ((row >> 4) & 1) * 256 + (row & 15) * 16 + (row >> 5)
    sc[...] = matmul(one_hot(source, 512), rc_in[...]).astype(bf16).reshape(32, 16, D)
    send_cotangent(0)
    for load in loads[4:]:
        load.wait()

    wait_bytes(ra, sem.at[1])
    send_cotangent(1)
    source = (((row >> 1) & 31) * 2 + ((row >> 6) & 1)) * 8 + (row & 1) * 4 + (row >> 7)
    ordered = matmul(one_hot(source, 512), ra[...].reshape(512, D)).astype(bf16)
    for piece in range(8):
        patch, half = piece // 2, piece % 2
        base[half, 64 * patch : 64 * patch + 64] = ordered[64 * piece : 64 * piece + 64]
    qkv[...] = matmul(rms_norm(ordered), project_ref[...]).astype(bf16)

    wait_bytes(rs, sem.at[3])
    for index in range(64):
        side[index : index + 1] = rs[index]
    side_low = side[...].astype(bf16)
    info = jnp.zeros((8, 128), f32)
    pick_row, pick_lane = iota((8, 128), 0), iota((8, 128), 1)
    for when in range(2):
        wanted = jnp.where(pick_row < 4, when * 16 + 4 * kk + pick_row, 32 + when + 2 * (pick_row - 4))
        picked = contract_last(jnp.where(pick_lane == wanted, 1.0, 0.0).astype(bf16), side_low)
        giver = iota((64, 128), 0)
        place = (giver & 1) * 64 + (giver >> 1) * 2 + when
        spread = jnp.where(iota((64, 128), 1) == place, 1.0, 0.0).astype(bf16)
        info = info + matmul(picked.astype(bf16), spread)
    info_ref[...] = info
    days = info[4:5] * 32.0 + info[5:6]
    same_date = iota((128, 128), 0) == iota((128, 128), 1)
    days_down = jnp.sum(jnp.where(same_date, days, 0.0), axis=1, keepdims=True)
    gap_ref[...] = jnp.abs(days_down - days)

    def time_patch(half, patch):
        rows = pl.ds(pl.multiple_of(patch * 128 + half * 64, 64), 64)
        keys_rows = pl.ds(pl.multiple_of(patch * 128, 128), 128)
        out_rows = pl.ds(pl.multiple_of(patch * 64, 64), 64)
        masks = head_masks()
        allowed = (info_ref[pl.ds(patch, 1), :] > 0.5) | (
            iota((64, 128), 0) + 64 * half == iota((64, 128), 1)
        )
        gap = gap_ref[pl.ds(pl.multiple_of(half * 64, 64), 64), :]
        for group in range(GROUPS):
            queries = qkv[rows, 128 * group : 128 * group + 128]
            keys = stacked(qkv[keys_rows, D + 128 * group : D + 128 * group + 128], masks)
            values = stacked(qkv[keys_rows, 2 * D + 128 * group : 2 * D + 128 * group + 128], masks)
            scores = contract_last(queries, keys)
            weights = []
            for head in range(4):
                block = scores[:, 128 * head : 128 * head + 128] * inverse_root
                block = block + (-slopes_ref[4 * group + head]) * gap
                block = jnp.where(allowed, block, masked_score)
                weights.append(softmax_block(block).astype(bf16))
            heads[out_rows, 128 * group : 128 * group + 128] = matmul(
                jnp.concatenate(weights, axis=1), values
            ).astype(bf16)

    slot = 4 * r + kk
    home = r == octet

    def time_half(half, carry):
        def time_pair(pair, inner):
            time_patch(half, 2 * pair)
            time_patch(half, 2 * pair + 1)
            return inner

        lax.fori_loop(0, 2, time_pair, 0)
        hidden = (
            base[half].astype(f32) + matmul(heads[0:256, :], output_ref[...])
        ).astype(bf16)
        small = iota((256, 1), 0)
        source = ((small >> 1) & 3) * 64 + (small >> 3) * 2 + (small & 1)
        sb[half] = matmul(one_hot(source, 256), hidden).astype(bf16).reshape(32, 8, D)

        def send_hidden(step, inner):
            to = lax.rem(lax.div(d, 2) + swing(step, 32), 32)
            remote(
                sb.at[half, to], rb_ref.at[half, slot], b_sem.at[half], b_sem.at[2 + half],
                (2 * to + parity, octet),
            ).start()
            return inner

        lax.fori_loop(1, 32, send_hidden, 0)

        @pl.when(home)
        def _():
            pltpu.make_async_copy(sb.at[half, d // 2], rb_ref.at[half, slot], b_sem.at[2 + half]).start()

        @pl.when(jnp.logical_not(home))
        def _():
            remote(
                sb.at[half, d // 2], rb_ref.at[half, slot], b_sem.at[half], b_sem.at[2 + half], (d, octet)
            ).start()

        return carry

    lax.fori_loop(0, 2, time_half, 0)

    wait_bytes(rc_ref, sem.at[5])
    heads_grad[...] = contract_last(rc_ref[...].reshape(512, D), column_output_ref[...]).astype(bf16)
    def column_date(date, carry):
        rows = pl.ds(pl.multiple_of(date * 128, 128), 128)
        masks = head_masks()
        for group in range(GROUPS):
            lanes = slice(128 * group, 128 * group + 128)
            queries = qkv[rows, 128 * group : 128 * group + 128]
            keys = stacked(qkv[rows, D + 128 * group : D + 128 * group + 128], masks)
            values = stacked(qkv[rows, 2 * D + 128 * group : 2 * D + 128 * group + 128], masks)
            outer = heads_grad[rows, lanes]
            scores = contract_last(queries, keys)
            products = contract_last(outer, values)
            weights_low, scores_low = [], []
            for head in range(4):
                weights = softmax_block(scores[:, 128 * head : 128 * head + 128], inverse_root)
                product = products[:, 128 * head : 128 * head + 128]
                centre = jnp.sum(weights * product, axis=-1, keepdims=True)
                weights_low.append(weights.astype(bf16))
                scores_low.append((weights * (product - centre)).astype(bf16))
            low = jnp.concatenate(weights_low, axis=1)
            score_low = jnp.concatenate(scores_low, axis=1)
            heads[rows, lanes] = matmul(low, values).astype(bf16)
            qkv_grad[rows, 128 * group : 128 * group + 128] = (
                matmul(score_low, keys) * inverse_root
            ).astype(bf16)
            qkv_grad[rows, D + 128 * group : D + 128 * group + 128] = (
                unstacked(contract_rows(score_low, queries), masks) * inverse_root
            ).astype(bf16)
            qkv_grad[rows, 2 * D + 128 * group : 2 * D + 128 * group + 128] = unstacked(
                contract_rows(low, outer), masks
            ).astype(bf16)
        return carry

    def send_mixed(date, carry):
        rows = pl.ds(pl.multiple_of(date * 128, 128), 128)
        mixed = plane[rows, :].astype(f32) + matmul(heads[rows, :], column_output_ref[...])
        send_c[date] = mixed.astype(bf16).reshape(8, 16, D)
        to_date = d - parity + date // 2

        def send_rows(step, inner):
            to = lax.rem(r + swing(step, 8), 8)
            remote(
                send_c.at[date, to], recv_c.at[date % 2, own], sem.at[8], sem.at[9], (to_date, to)
            ).start()
            return inner

        lax.fori_loop(1, 8, send_rows, 0)

        @pl.when(to_date == d)
        def _():
            pltpu.make_async_copy(send_c.at[date, r], recv_c.at[date % 2, own], sem.at[9]).start()

        @pl.when(to_date != d)
        def _():
            remote(
                send_c.at[date, r], recv_c.at[date % 2, own], sem.at[8], sem.at[9], (to_date, r)
            ).start()

        return carry

    def column_half(half, carry):
        wait_bytes(rb_ref.at[half], b_sem.at[2 + half])
        rows = pl.ds(pl.multiple_of(half * 256, 256), 256)
        small = iota((256, 1), 0)
        source = (small & 127) * 2 + (small >> 7)
        hidden = matmul(one_hot(source, 256), rb_ref[half].reshape(256, D)).astype(bf16)
        plane[rows, :] = hidden
        column_normed = rms_norm(hidden)
        normed[rows, :] = column_normed
        qkv[rows, :] = matmul(column_normed, column_project_ref[...]).astype(bf16)
        lax.fori_loop(2 * half, 2 * half + 2, column_date, 0)

        @pl.when(half == 0)
        def _():
            lax.fori_loop(0, 2, send_mixed, 0)

        return carry

    lax.fori_loop(0, 2, column_half, 0)

    natural[0:1152] = contract_rows(qkv_grad[...], normed[...])
    natural[1152:1536] = contract_rows(rc_ref[...].reshape(512, D), heads[...])
    for block in range(64):
        bits = (block % 8) * 8 + (block // 32) * 4 + (block // 8) % 4
        flipped_block = (block // 32) * 32 + (block % 8) * 4 + (block // 8) % 4
        partial_y[flipped_block, 0:18] = natural[18 * bits : 18 * bits + 18, 256:384]
        partial_y[flipped_block, 18:24] = natural[1152 + 6 * bits : 1152 + 6 * bits + 6, 256:384]
        partial_x[block, 0:18] = natural[18 * bits : 18 * bits + 18, 0:256]
        partial_x[block, 18:24] = natural[1152 + 6 * bits : 1152 + 6 * bits + 6, 0:256]

    along_x = (x, 4, 1, (1, 3, 2), lambda step: (d - x + (x + step) % 4, r))
    along_y = (octet, 8, 8, (1, 7, 2, 6, 3, 5, 4), lambda step: ((d + 8 * step) % 64, r))
    plans = (
        (2, partial_y, 0, along_y, s2y, r2y, along_x, s3y, r3y),
        (0, partial_x, 0, along_x, s2x.at[0], r2x.at[0], along_y, s3x.at[0], r3x.at[0]),
        (1, partial_x, 128, along_x, s2x.at[1], r2x.at[1], along_y, s3x.at[1], r3x.at[1]),
    )

    def exchange(axis, sent, received, send_sem, recv_sem):
        me, size, _, steps, device = axis
        for step in steps:
            remote(
                sent.at[(me + step) % size], received.at[step - 1], send_sem, recv_sem, device(step)
            ).start()

    def gathered(axis, sent, received, recv_sem):
        me, size = axis[:2]
        wait_bytes(received, recv_sem)
        total = sent[me].astype(f32)
        for index in range(size - 1):
            total = total + received[index].astype(f32)
        return total

    for chunk, partial, low, *_ in plans:
        other = partial[pl.ds(pl.multiple_of(32 - 32 * core, 32), 32), :, low : low + 128]
        s1[chunk] = other.reshape(768, 128).astype(bf16)
        remote(
            s1.at[chunk], r1.at[chunk], grad_sem.at[chunk], grad_sem.at[3 + chunk], partner
        ).start()
    for chunk, partial, low, first_axis, sent, received, *_ in plans:
        mine = partial[pl.ds(pl.multiple_of(32 * core, 32), 32), :, low : low + 128].reshape(768, 128)
        wait_bytes(r1.at[chunk], grad_sem.at[3 + chunk])
        size = first_axis[1]
        sent[...] = (mine + r1[chunk].astype(f32)).astype(bf16).reshape(size, 768 // size, 128)
        exchange(first_axis, sent, received, grad_sem.at[6 + chunk], grad_sem.at[9 + chunk])
    lax.fori_loop(2, 4, send_mixed, 0)
    for chunk, _, _, first_axis, sent, received, second_axis, sent_next, received_next in plans:
        total = gathered(first_axis, sent, received, grad_sem.at[9 + chunk])
        sent_next[...] = total.reshape(second_axis[1], 24, 128).astype(bf16)
        exchange(
            second_axis, sent_next, received_next, grad_sem.at[12 + chunk], grad_sem.at[15 + chunk]
        )
    for chunk, _, _, _, _, _, second_axis, sent_next, received_next in plans:
        total = gathered(second_axis, sent_next, received_next, grad_sem.at[15 + chunk])
        square = jnp.concatenate([total, jnp.zeros((104, 128), f32)], axis=0)
        s4[128 * chunk : 128 * chunk + 128] = jnp.transpose(square).astype(bf16)
    z_slot = (r // 2) * 2 + z_lo
    final_date = d - 4 * z_lo + 4 * core

    def send_final(step, carry):
        to = (r + swing(step, 8)) % 8
        remote(
            s4.at[pl.ds(pl.multiple_of(48 * to, 16), 48)], r4.at[z_slot],
            grad_sem.at[18], grad_sem.at[19], (final_date, to),
        ).start()
        return carry

    lax.fori_loop(1, 8, send_final, 0)
    mine_last = s4.at[pl.ds(pl.multiple_of(48 * r, 16), 48)]

    @pl.when(final_date == d)
    def _():
        pltpu.make_async_copy(mine_last, r4.at[z_slot], grad_sem.at[19]).start()

    @pl.when(final_date != d)
    def _():
        remote(
            mine_last, r4.at[z_slot], grad_sem.at[18], grad_sem.at[19], (final_date, r)
        ).start()

    wait_bytes(sa.at[pl.ds(0, 63)], sem.at[0])
    wait_bytes(rs.at[pl.ds(0, 63)], sem.at[2])
    wait_bytes(sc.at[pl.ds(0, 30)], sem.at[4])
    for half in range(2):
        wait_bytes(sb.at[half, pl.ds(0, 31)], b_sem.at[half])

    @pl.when(jnp.logical_not(home))
    def _():
        for half in range(2):
            wait_bytes(sb.at[half, 0], b_sem.at[half])

    wait_bytes(send_c.at[pl.ds(0, 3)], sem.at[8])
    wait_bytes(send_c.at[3, pl.ds(0, 6)], sem.at[8])
    for chunk, _, _, first_axis, sent, received, second_axis, sent_next, received_next in plans:
        wait_bytes(s1.at[chunk], grad_sem.at[chunk])
        wait_bytes(received, grad_sem.at[6 + chunk])
        wait_bytes(received_next, grad_sem.at[12 + chunk])
    wait_bytes(recv_c, sem.at[9])
    wait_bytes(r4, grad_sem.at[19])
    wait_bytes(r4.at[pl.ds(0, 7)], grad_sem.at[18])

    @pl.when(final_date != d)
    def _():
        wait_bytes(r4.at[0], grad_sem.at[18])


def finish_kernel(recv_c, r4, mixed_ref, project_grad_ref, output_grad_ref):
    small = iota((256, 1), 0)
    order = one_hot((small & 15) * 16 + (small >> 4), 256)
    for when in range(2):
        mixed_ref[256 * when : 256 * when + 256] = matmul(
            order, recv_c[when].reshape(256, D)
        ).astype(bf16)
    total = r4[0].astype(f32)
    for index in range(1, 8):
        total = total + r4[index].astype(f32)
    turned = jnp.transpose(jnp.concatenate([total, jnp.zeros((80, 128), f32)], axis=0))
    project_grad_ref[...] = turned[0:18, 0:48]
    output_grad_ref[...] = turned[18:24, 0:48]


VM = pl.BlockSpec(memory_space=pltpu.VMEM)
HB = pl.BlockSpec(memory_space=pltpu.HBM)


def body(
    tokens, clear_flags, date_numbers, decay_slopes, time_project, time_output,
    column_project, column_output, cotangent,
):
    vmem = pltpu.VMEM
    recv_c, r4 = pl.pallas_call(
        layer_kernel,
        out_shape=(
            jax.ShapeDtypeStruct((2, 16, 16, D), bf16),
            jax.ShapeDtypeStruct((8, 48, 128), bf16),
        ),
        in_specs=[HB] * 9,
        out_specs=(VM, VM),
        scratch_shapes=[
            vmem((512, D), bf16),
            vmem((512, D), bf16),
            vmem((32, 16), jnp.int32),
            vmem((D, 3 * D), bf16),
            vmem((D, D), bf16),
            vmem((D, 3 * D), bf16),
            vmem((D, D), bf16),
            pltpu.SMEM((2,), jnp.int32),
            pltpu.SMEM((HEADS,), f32),
            vmem((64, 8, D), bf16),
            vmem((64, 8, D), bf16),
            vmem((16, 1, 128), f32),
            vmem((64, 1, 128), f32),
            vmem((32, 16, D), bf16),
            vmem((2, 32, 8, D), bf16),
            vmem((2, 32, 8, D), bf16),
            vmem((4, 128, D), bf16),
            vmem((64, 128), f32),
            vmem((128, 128), f32),
            vmem((8, 128), f32),
            vmem((2, 256, D), bf16),
            vmem((512, 3 * D), bf16),
            vmem((512, D), bf16),
            vmem((512, D), bf16),
            vmem((512, D), bf16),
            vmem((512, D), bf16),
            vmem((512, 3 * D), bf16),
            vmem((4, 8, 16, D), bf16),
            vmem((1536, D), f32),
            vmem((64, 24, 256), f32),
            vmem((64, 24, 128), f32),
            vmem((3, 768, 128), bf16),
            vmem((3, 768, 128), bf16),
            vmem((2, 4, 192, 128), bf16),
            vmem((2, 3, 192, 128), bf16),
            vmem((2, 8, 24, 128), bf16),
            vmem((2, 7, 24, 128), bf16),
            vmem((8, 96, 128), bf16),
            vmem((7, 96, 128), bf16),
            vmem((4, 24, 128), bf16),
            vmem((3, 24, 128), bf16),
            vmem((D, 128), bf16),
            pltpu.SemaphoreType.DMA((10,)),
            pltpu.SemaphoreType.DMA((20,)),
            pltpu.SemaphoreType.DMA((9,)),
            pltpu.SemaphoreType.DMA((4,)),
        ],
        compiler_params=pltpu.CompilerParams(
            collective_id=0, has_side_effects=True, vmem_limit_bytes=48 * 1024 * 1024
        ),
        name="layer",
    )(
        *(
            pltpu.with_memory_space_constraint(value, pltpu.HBM)
            for value in (
                tokens.reshape(512, D), cotangent.reshape(512, D), clear_flags.reshape(32, 16),
                time_project, time_output, column_project, column_output, date_numbers, decay_slopes,
            )
        )
    )
    mixed, project_grad, output_grad = pl.pallas_call(
        finish_kernel,
        out_shape=(
            jax.ShapeDtypeStruct((512, D), bf16),
            jax.ShapeDtypeStruct((18, 48), f32),
            jax.ShapeDtypeStruct((6, 48), f32),
        ),
        in_specs=[VM] * 2,
        out_specs=(VM, VM, VM),
        compiler_params=pltpu.CompilerParams(vmem_limit_bytes=8 * 1024 * 1024),
        name="finish",
    )(recv_c, r4)
    return mixed.reshape(tokens.shape), project_grad.T, output_grad.T


def solution(mesh):
    return jax.shard_map(
        body,
        mesh=mesh,
        in_specs=(
            P("date", "row", None, None), P("date", "row", None), P("date"),
            P(), P(), P(), P(), P(), P("date", "row", None, None),
        ),
        out_specs=(P("date", "row", None, None), P("row", "date"), P("row", "date")),
        check_vma=False,
    )
```
